512 devices in a mesh: rep: 16 (over x, z_lo), shard: 32 (over y, z_hi, core).
Axes of the slice: x: 4, y: 8, z: 8 (z_hi: 2, z_lo: 4; z = z_hi * 4 + z_lo), core: 2. Of those that a mesh axis runs over, the one named last changes fastest.
Arguments:
- queries: bfloat16 [16, 4096, 2048], P('rep', 'shard'), may hold values from -6 to 6
- keys: bfloat16 [16, 4096, 256], P('rep', 'shard'), may hold values from -6 to 6
- values: bfloat16 [16, 4096, 256], P('rep', 'shard'), may hold values from -6 to 6
- segments: int32 [16, 4096], P('rep', 'shard'), may hold values from 0 to 63, never falling along the last dimension, each value on 1 to 512 neighbouring positions
- grad_output: bfloat16 [16, 4096, 1024], P('rep', 'shard'), may hold values from -0.125 to 0.125
Outputs:
- attention: bfloat16 [16, 4096, 2048], P('rep', 'shard')
- grad_weight: float32 [1024, 2048], P('shard')
The draws below stay inside these ranges and needn't reach their ends.
Inputs may be any that keep to these rules, and one draw needn't show every extreme that they name: `segments`: document numbers never fall along a packed row; every document holds 1 to 512 positions and some document holds exactly 512.
All inputs are finite; a program needn't handle non-finite values.
Results may differ from the reference program's by a relative error of at most 0.015.
Values may be sent and summed in bfloat16 or wider, within the bound.
No kernel may reach another device: no remote copies, remote signals or barrier semaphores. Data moves between devices by JAX's collectives and lax.ppermute only.
A program may use at most 64 MiB of HBM per device.

```python
import math
import jax
import jax.numpy as jnp
import numpy as np
from jax import lax

HEADS = 16
KVH = 2
HD = 128
D_WIN = 1024
TOK_DEV = 128
MOST = 512
SEQ = 4096
BATCH = 16
DOCS = 64
N_SHARD = 32


def draw_queries(key, part):
    shape_full = (BATCH, SEQ, HEADS * HD)
    base = jax.random.normal(jax.random.fold_in(key, 22), shape_full, jnp.float32)
    return jnp.clip(base, -6.0, 6.0).astype(jnp.bfloat16)


def draw_keys(key, part):
    shape_full = (BATCH, SEQ, KVH * HD)
    base = jax.random.normal(jax.random.fold_in(key, 32), shape_full, jnp.float32)
    return jnp.clip(base, -6.0, 6.0).astype(jnp.bfloat16)


def with_spikes(drawn, stream_key, source, target, blocks, factor):
    owner, partner = [(jnp.arange(drawn.shape[axis_at]) // (drawn.shape[axis_at] // blocks)).reshape([-1 if axis == axis_at else 1 for axis in range(drawn.ndim)]) for axis_at in (source, target)]
    chosen = jax.random.permutation(stream_key, blocks)[partner]
    strong = (owner == chosen) | (owner == (partner + blocks // 2) % blocks)
    return jnp.where(strong, factor * drawn, drawn)


def shard_levels(rng, dims, split, least, largest):
    def one(axis_at, shards_of):
        draws = jax.random.uniform(jax.random.fold_in(jax.random.fold_in(rng, 6), axis_at), (shards_of,), jnp.float32, least / len(split), largest / len(split))
        return jnp.repeat(jnp.exp(draws), dims[axis_at] // shards_of).reshape((-1,) + (1,) * (len(dims) - axis_at - 1))

    gain = one(*split[0])
    for cut in split[1:]:
        gain = gain * one(*cut)
    return gain


def length_profile(amount, total, reach, lean):
    portions = [(1 << 20) // math.isqrt(standing ** lean) + 1 for standing in range(2, amount + 1)]
    rest, given = total - reach - (amount - 1), [1] * (amount - 1)
    while rest > 0:
        movable = [i for i in range(amount - 1) if given[i] < reach]
        mass, left = sum([portions[i] for i in movable]), rest
        for i in movable:
            extra = min(reach - given[i], max(1, left * portions[i] // mass), rest)
            given[i] = given[i] + extra
            rest = rest - extra
    return np.array([reach] + given)


def ragged(stream_key, count, total, reach, lean):
    if count == 2:
        one = jax.random.randint(stream_key, (), max(1, total - reach), min(reach, total - 1) + 1)
        return jnp.stack([one, total - one])
    tallies = jnp.asarray(length_profile(count, total, reach, lean), jnp.int32)
    couples = (count - 1) // 2
    source_of, receiver = tallies[1:1 + 2 * couples:2], tallies[2:2 + 2 * couples:2]
    margin = jnp.minimum(source_of - 1, reach - receiver)
    passed = jax.random.randint(jax.random.fold_in(stream_key, 1), (couples,), 0, 1 << 20) % (margin + 1)
    tallies = tallies.at[1:1 + 2 * couples:2].set(source_of - passed).at[2:2 + 2 * couples:2].set(receiver + passed)
    return tallies[jax.random.permutation(jax.random.fold_in(stream_key, 2), count)]


def centred(key, dims, deviation, most, split=(), kind=jnp.bfloat16):
    result = jax.random.normal(key, dims, jnp.float32) * deviation
    if len(split) > 0:
        result = shard_levels(key, dims, split, -0.22, 0.18) * result
    return jnp.clip(result, min=-most, max=most).astype(kind)


def bell_draw_with(stream_key, shape, width, limit, pieces, heavy, kind=jnp.bfloat16):
    entries = width * jax.random.normal(stream_key, shape, jnp.float32)
    if pieces:
        entries = entries * shard_levels(stream_key, shape, pieces, -0.22, 0.18)
    return jnp.clip(with_spikes(entries, jax.random.fold_in(stream_key, 3), *heavy), -limit, limit).astype(kind)


def setup_inputs(seed: int = 0) -> dict:
    splits = jax.random.split(jax.random.key(seed), 6)
    queries = draw_queries(jax.random.fold_in(splits[5], 71), 0)
    keys = draw_keys(jax.random.fold_in(splits[5], 71), 0)
    values = centred(splits[2], (BATCH, SEQ, KVH * HD), 1.0, 6.0, ((0, 16), (1, 32)))
    segments = jax.vmap(lambda own: jnp.searchsorted(jnp.cumsum(ragged(own, DOCS, SEQ, MOST, 2)), jnp.arange(SEQ), side="right"))(jax.random.split(splits[3], BATCH)).reshape((BATCH, SEQ)).astype(jnp.int32)
    grad_output = bell_draw_with(splits[4], (BATCH, SEQ, D_WIN), (3.0 / (BATCH * SEQ) ** 0.5), 0.125, ((0, 16), (1, 32)), (1, 2, 32, 2.75))
    return dict(queries=queries, keys=keys, values=values, segments=segments, grad_output=grad_output)


def attend_row(queries_row, keys_row, values_row, segment_row):
    block_rows = min(512, SEQ)
    window = min(block_rows + MOST, SEQ)
    group_size = HEADS // KVH

    def one_block(block_index):
        q_first = (block_index * block_rows).astype(jnp.int32)
        k_first = jnp.clip(q_first + block_rows - window, 0, SEQ - window).astype(jnp.int32)
        q_block = lax.dynamic_slice_in_dim(queries_row, q_first, block_rows, 0).astype(jnp.float32)
        q_block = q_block.reshape(block_rows, KVH, group_size, HD)
        k_block = lax.dynamic_slice_in_dim(keys_row, k_first, window, 0).astype(jnp.float32).reshape(window, KVH, HD)
        v_block = lax.dynamic_slice_in_dim(values_row, k_first, window, 0).astype(jnp.float32).reshape(window, KVH, HD)
        q_seg = lax.dynamic_slice_in_dim(segment_row, q_first, block_rows, 0)
        k_seg = lax.dynamic_slice_in_dim(segment_row, k_first, window, 0)
        q_pos = q_first + jnp.arange(block_rows, dtype=jnp.int32)
        k_pos = k_first + jnp.arange(window, dtype=jnp.int32)
        allowed = (q_seg[:, None] == k_seg[None, :]) & (k_pos[None, :] <= q_pos[:, None])
        scores = jnp.einsum("qhgd,khd->hgqk", q_block, k_block) * (HD ** -0.5)
        scores = jnp.where(allowed, scores, -1e30)
        row_max = jnp.max(scores, axis=-1, keepdims=True)
        weights = jnp.where(allowed, jnp.exp(scores - row_max), 0.0)
        denominator = jnp.sum(weights, axis=-1)
        mixed = jnp.einsum("hgqk,khd->hgqd", weights, v_block, precision=lax.Precision.HIGHEST)
        mixed = mixed / denominator[..., None]
        output_rows = jnp.transpose(mixed, (2, 0, 1, 3)).reshape(block_rows, HEADS * HD)
        return output_rows.astype(jnp.bfloat16)

    blocks = lax.map(one_block, jnp.arange(SEQ // block_rows, dtype=jnp.int32))
    return blocks.reshape(SEQ, HEADS * HD)


def row_attention(row_data):
    return attend_row(*row_data)


def reference(queries, keys, values, segments, grad_output):
    attention = lax.map(row_attention, (queries, keys, values, segments))
    flat_attn = attention.reshape(BATCH * N_SHARD, TOK_DEV, HEADS * HD)
    flat_grad = grad_output.reshape(BATCH * N_SHARD, TOK_DEV, D_WIN)

    def add_block(running, pair):
        partial_value = lax.dot_general(pair[1], pair[0], (((0,), (0,)), ((), ())), preferred_element_type=jnp.float32)
        rounded = lax.optimization_barrier(partial_value.astype(jnp.bfloat16))
        return running + rounded.astype(jnp.float32), None

    grad_weight, unused = lax.scan(add_block, jnp.zeros((D_WIN, HEADS * HD), jnp.float32), (flat_attn, flat_grad))
    return attention, grad_weight
```

```python
import jax
import jax.numpy as jnp
import numpy as np
from jax import lax
from jax.experimental import pallas as pl
from jax.experimental.pallas import tpu as pltpu
from jax.sharding import Mesh
from jax.sharding import PartitionSpec as P

HEADS = 16
KVH = 2
HD = 128
TOK = 128
D_WIN = 1024
SPAN = 4
N_SHARD = 32
N_REP = 16
KV = KVH * HD
PAY_ROWS = TOK + 8
NEG = -1e30
EXP2_SCALE = (HD**-0.5) * 1.4426950408889634

AXES = ("x", "zlh", "zll", "shard")
REP = ("x", "zlh", "zll")
GROUP = ("x", "zll")
N_GROUP = 8
REST = ("shard", "zlh")
N_REST = 64
STACK = 4


def params(mib):
    return pltpu.CompilerParams(vmem_limit_bytes=mib << 20)


def vmem_specs(count):
    return [pl.BlockSpec(memory_space=pltpu.VMEM)] * count


def pack_kernel(key_ref, value_ref, seg_ref, grad_ref, pay_ref, grad_t_ref):
    pay_ref[:TOK, :KV] = key_ref[0]
    pay_ref[:TOK, KV:] = value_ref[0]
    seg = jnp.broadcast_to(seg_ref[...].astype(jnp.float32), (8, TOK))
    pay_ref[TOK:, :TOK] = seg.astype(jnp.bfloat16)
    pay_ref[TOK:, TOK:] = jnp.zeros((8, 2 * KV - TOK), jnp.bfloat16)
    grad_t_ref[...] = jnp.transpose(grad_ref[0].astype(jnp.float32)).astype(jnp.bfloat16)


def pack(keys, values, segments, grad_output):
    return pl.pallas_call(
        pack_kernel,
        out_shape=(
            jax.ShapeDtypeStruct((PAY_ROWS, 2 * KV), jnp.bfloat16),
            jax.ShapeDtypeStruct((D_WIN, TOK), jnp.bfloat16),
        ),
        in_specs=vmem_specs(4),
        out_specs=tuple(vmem_specs(2)),
        name="pack",
        compiler_params=params(8),
        cost_estimate=pl.CostEstimate(flops=0, bytes_accessed=1 << 20, transcendentals=0),
    )(keys, values, segments, grad_output)


def attend_kernel(index_ref, query_ref, *refs):
    pays, (out_ref, swap_ref, bias_ref) = refs[: SPAN + 1], refs[SPAN + 1 :]
    index = index_ref[0]
    own_row = jnp.broadcast_to(pays[0][TOK : TOK + 1, :TOK].astype(jnp.float32), (TOK, TOK))
    q_seg = jnp.transpose(own_row)
    q_at = lax.broadcasted_iota(jnp.int32, (TOK, TOK), 0)
    k_at = lax.broadcasted_iota(jnp.int32, (TOK, TOK), 1)
    for step in range(SPAN + 1):
        k_seg = jnp.broadcast_to(pays[step][TOK : TOK + 1, :TOK].astype(jnp.float32), (TOK, TOK))
        allowed = q_seg == k_seg
        if step == 0:
            allowed = allowed & (k_at <= q_at)
        else:
            allowed = allowed & (k_at + (index - step) * TOK >= 0)
        bias_ref[:, step * TOK : (step + 1) * TOK] = jnp.where(allowed, 0.0, NEG)
    ones = jnp.ones((TOK, HD), jnp.bfloat16)
    for first in range(0, HEADS, STACK):
        kv_head = first // (HEADS // KVH)
        k_cols = slice(kv_head * HD, (kv_head + 1) * HD)
        v_cols = slice(KV + kv_head * HD, KV + (kv_head + 1) * HD)
        query = jnp.concatenate(
            [query_ref[0, :, h * HD : (h + 1) * HD] for h in range(first, first + STACK)], axis=0
        )
        key = jnp.concatenate([pay[:TOK, k_cols] for pay in pays], axis=0)
        scores = lax.dot_general(
            query, key, (((1,), (1,)), ((), ())), preferred_element_type=jnp.float32
        )
        bias = bias_ref[...]
        scores = scores.reshape(STACK, TOK, (SPAN + 1) * TOK) + bias[None]
        largest = jnp.max(scores, axis=-1, keepdims=True)
        weights = jnp.exp2((scores - largest) * EXP2_SCALE).astype(jnp.bfloat16)
        weights = weights.reshape(STACK * TOK, (SPAN + 1) * TOK)
        value = jnp.concatenate(
            [jnp.concatenate([pay[:TOK, v_cols], ones], axis=1) for pay in pays], axis=0
        )
        mixed = jnp.dot(weights, value, preferred_element_type=jnp.float32)
        result = (mixed[:, :HD] / mixed[:, HD:]).astype(jnp.bfloat16)
        for h in range(STACK):
            head = first + h
            rows = result[h * TOK : (h + 1) * TOK]
            out_ref[0, :, head * HD : (head + 1) * HD] = rows
            swap_ref[head // 2, :, (head % 2) * HD : (head % 2 + 1) * HD] = rows


def attend(index, queries, pays):
    return pl.pallas_call(
        attend_kernel,
        out_shape=(
            jax.ShapeDtypeStruct((1, TOK, HEADS * HD), jnp.bfloat16),
            jax.ShapeDtypeStruct((N_GROUP, TOK, 2 * HD), jnp.bfloat16),
        ),
        in_specs=[pl.BlockSpec(memory_space=pltpu.SMEM)] + vmem_specs(SPAN + 2),
        out_specs=tuple(vmem_specs(2)),
        scratch_shapes=[pltpu.VMEM((TOK, (SPAN + 1) * TOK), jnp.float32)],
        name="attend",
        compiler_params=params(32),
        cost_estimate=pl.CostEstimate(
            flops=700_000_000, bytes_accessed=3 << 20, transcendentals=1_310_720
        ),
    )(index, queries, *pays)


def term_kernel(grad_t_ref, mixed_ref, out_ref):
    grad_t = jnp.concatenate([grad_t_ref[i] for i in range(N_GROUP)], axis=1)
    mixed = mixed_ref[...].reshape(N_GROUP * TOK, 2 * HD)
    term = jnp.dot(grad_t, mixed, preferred_element_type=jnp.float32).astype(jnp.bfloat16)
    term = term.reshape(N_SHARD, D_WIN // N_SHARD, 2 * HD)
    for half in range(2):
        out_ref[:, half] = term[:, :, half * HD : (half + 1) * HD]


def weight_term(grad_t, mixed):
    return pl.pallas_call(
        term_kernel,
        out_shape=jax.ShapeDtypeStruct((N_SHARD, 2, D_WIN // N_SHARD, HD), jnp.bfloat16),
        in_specs=vmem_specs(2),
        out_specs=vmem_specs(1)[0],
        name="weight_term",
        compiler_params=params(24),
        cost_estimate=pl.CostEstimate(
            flops=2 * D_WIN * N_GROUP * TOK * 2 * HD, bytes_accessed=3 << 20, transcendentals=0
        ),
    )(grad_t, mixed)


def total_kernel(terms_ref, out_ref):
    total = jnp.sum(terms_ref[...].astype(jnp.float32), axis=0).astype(jnp.bfloat16)
    out_ref[...] = jnp.broadcast_to(total[None], out_ref.shape)


def total(terms):
    return pl.pallas_call(
        total_kernel,
        out_shape=jax.ShapeDtypeStruct((N_REP, D_WIN // N_SHARD, HD), jnp.bfloat16),
        in_specs=vmem_specs(1),
        out_specs=vmem_specs(1)[0],
        name="total",
        compiler_params=params(8),
    )(terms)


def assemble_kernel(parts_ref, out_ref):
    for x in range(4):
        for zlh in range(2):
            for zll in range(2):
                head = (x * 2 + zll) * 2 + zlh
                part = parts_ref[x * 4 + zlh * 2 + zll]
                out_ref[:, head * HD : (head + 1) * HD] = part.astype(jnp.float32)


def assemble(parts):
    return pl.pallas_call(
        assemble_kernel,
        out_shape=jax.ShapeDtypeStruct((D_WIN // N_SHARD, HEADS * HD), jnp.float32),
        in_specs=vmem_specs(1),
        out_specs=vmem_specs(1)[0],
        name="assemble",
        compiler_params=params(8),
    )(parts)


def shifted(value, steps):
    count = lax.axis_size("shard")
    return lax.ppermute(value, "shard", [(s, s + steps) for s in range(count - steps)])


def local(queries, keys, values, segments, grad_output):
    pay, grad_t = pack(keys, values, segments, grad_output)
    grads = lax.all_gather(grad_t, GROUP, axis=0, tiled=False)
    pays = [pay] + [shifted(pay, step) for step in range(1, SPAN + 1)]
    index = lax.axis_index("shard").reshape(1).astype(jnp.int32)
    attention, swap = attend(index, queries, pays)
    mixed = lax.all_to_all(swap, GROUP, 0, 0, tiled=True)
    term = weight_term(grads.reshape(N_GROUP, D_WIN, TOK), mixed)
    terms = lax.all_to_all(
        term.reshape(N_REST, D_WIN // N_SHARD, HD), REST, 0, 0, tiled=True
    )
    parts = lax.all_to_all(total(terms), REP, 0, 0, tiled=True)
    return attention, assemble(parts)


def solution(mesh):
    fine = Mesh(np.asarray(mesh.devices).reshape(4, 2, 2, N_SHARD), AXES)
    row = P(REP, "shard", None)
    return jax.shard_map(
        local,
        mesh=fine,
        in_specs=(row, row, row, P(REP, "shard"), row),
        out_specs=(row, P("shard", None)),
        check_vma=False,
    )
```

```python
import jax
import jax.numpy as jnp
import numpy as np
from jax import lax
from jax.experimental import pallas as pl
from jax.experimental.pallas import tpu as pltpu
from jax.sharding import Mesh
from jax.sharding import PartitionSpec as P


HEADS = 16
KVH = 2
HD = 128
TOK = 128
D_WIN = 1024
SPAN = 4
N_SHARD = 32
N_REP = 16
KV = KVH * HD
PAY_ROWS = TOK + 8
NEG = -1e30
EXP2_SCALE = (HD**-0.5) * 1.4426950408889634

AXES = ("x", "zlh", "zll", "yz", "core")
SIZES = (4, 2, 2, 16, 2)
REP = ("x", "zlh", "zll")
SHARD = ("yz", "core")
GROUP = ("x", "zll")
N_X = 4
N_GROUP = 8
REST = ("yz", "zlh")
N_YZ = 16
N_REST = 32
ROWS = D_WIN // N_SHARD
HALF = D_WIN // 2
STACK = 4


def params(mib):
    return pltpu.CompilerParams(vmem_limit_bytes=mib << 20)


def vmem_specs(count):
    return [pl.BlockSpec(memory_space=pltpu.VMEM)] * count


def pack_kernel(core_ref, key_ref, value_ref, seg_ref, grad_ref, pay_ref, keep_ref, send_ref):
    pay_ref[:TOK, :KV] = key_ref[0]
    pay_ref[:TOK, KV:] = value_ref[0]
    seg = jnp.broadcast_to(seg_ref[...].astype(jnp.float32), (8, TOK))
    pay_ref[TOK:, :TOK] = seg.astype(jnp.bfloat16)
    pay_ref[TOK:, TOK:] = jnp.zeros((8, 2 * KV - TOK), jnp.bfloat16)
    grad_t = jnp.transpose(grad_ref[0].astype(jnp.float32)).reshape(N_YZ, 2, ROWS, TOK)
    even = grad_t[:, 0].reshape(HALF, TOK)
    odd = grad_t[:, 1].reshape(HALF, TOK)
    first = core_ref[0] == 0
    keep_ref[...] = jnp.where(first, even, odd).astype(jnp.bfloat16)
    send_ref[...] = jnp.where(first, odd, even).astype(jnp.bfloat16)


def pack(core, keys, values, segments, grad_output):
    return pl.pallas_call(
        pack_kernel,
        out_shape=(
            jax.ShapeDtypeStruct((PAY_ROWS, 2 * KV), jnp.bfloat16),
            jax.ShapeDtypeStruct((HALF, TOK), jnp.bfloat16),
            jax.ShapeDtypeStruct((HALF, TOK), jnp.bfloat16),
        ),
        in_specs=[pl.BlockSpec(memory_space=pltpu.SMEM)] + vmem_specs(4),
        out_specs=tuple(vmem_specs(3)),
        name="pack",
        cost_estimate=pl.CostEstimate(flops=0, bytes_accessed=1 << 20, transcendentals=0),
    )(core, keys, values, segments, grad_output)


def attend_kernel(index_ref, query_ref, *refs):
    pays, (out_ref, swap_ref, bias_ref) = refs[: SPAN + 1], refs[SPAN + 1 :]
    index = index_ref[0]
    own_row = jnp.broadcast_to(pays[0][TOK : TOK + 1, :TOK].astype(jnp.float32), (TOK, TOK))
    q_seg = jnp.transpose(own_row)
    q_at = lax.broadcasted_iota(jnp.int32, (TOK, TOK), 0)
    k_at = lax.broadcasted_iota(jnp.int32, (TOK, TOK), 1)
    for step in range(SPAN + 1):
        k_seg = jnp.broadcast_to(pays[step][TOK : TOK + 1, :TOK].astype(jnp.float32), (TOK, TOK))
        allowed = q_seg == k_seg
        if step == 0:
            allowed = allowed & (k_at <= q_at)
        else:
            odd = lax.rem(index, 2)
            back = (0, 2, 4, 3 - 2 * odd, 1 + 2 * odd)[step]
            allowed = allowed & (k_at + (index - back) * TOK >= 0)
        bias_ref[:, step * TOK : (step + 1) * TOK] = jnp.where(allowed, 0.0, NEG)
    ones = jnp.ones((TOK, HD), jnp.bfloat16)
    for first in range(0, HEADS, STACK):
        kv_head = first // (HEADS // KVH)
        k_cols = slice(kv_head * HD, (kv_head + 1) * HD)
        v_cols = slice(KV + kv_head * HD, KV + (kv_head + 1) * HD)
        query = jnp.concatenate(
            [query_ref[0, :, h * HD : (h + 1) * HD] for h in range(first, first + STACK)], axis=0
        )
        key = jnp.concatenate([pay[:TOK, k_cols] for pay in pays], axis=0)
        scores = lax.dot_general(
            query, key, (((1,), (1,)), ((), ())), preferred_element_type=jnp.float32
        )
        bias = bias_ref[...]
        scores = scores.reshape(STACK, TOK, (SPAN + 1) * TOK) + bias[None]
        largest = jnp.max(scores, axis=-1, keepdims=True)
        weights = jnp.exp2((scores - largest) * EXP2_SCALE).astype(jnp.bfloat16)
        weights = weights.reshape(STACK * TOK, (SPAN + 1) * TOK)
        value = jnp.concatenate(
            [jnp.concatenate([pay[:TOK, v_cols], ones], axis=1) for pay in pays], axis=0
        )
        mixed = jnp.dot(weights, value, preferred_element_type=jnp.float32)
        result = (mixed[:, :HD] / mixed[:, HD:]).astype(jnp.bfloat16)
        for h in range(STACK):
            head = first + h
            rows = result[h * TOK : (h + 1) * TOK]
            out_ref[0, :, head * HD : (head + 1) * HD] = rows
            swap_ref[head // 2, :, (head % 2) * HD : (head % 2 + 1) * HD] = rows


def attend(index, queries, pays):
    return pl.pallas_call(
        attend_kernel,
        out_shape=(
            jax.ShapeDtypeStruct((1, TOK, HEADS * HD), jnp.bfloat16),
            jax.ShapeDtypeStruct((N_GROUP, TOK, 2 * HD), jnp.bfloat16),
        ),
        in_specs=[pl.BlockSpec(memory_space=pltpu.SMEM)] + vmem_specs(SPAN + 2),
        out_specs=tuple(vmem_specs(2)),
        scratch_shapes=[pltpu.VMEM((TOK, (SPAN + 1) * TOK), jnp.float32)],
        name="attend",
        compiler_params=params(32),
        cost_estimate=pl.CostEstimate(
            flops=700_000_000, bytes_accessed=3 << 20, transcendentals=1_310_720
        ),
    )(index, queries, *pays)


def term_kernel(place_ref, *refs):
    grads, (mine_ref, other_ref, out_ref) = refs[:N_X], refs[N_X:]
    x, zll = place_ref[0], place_ref[1]
    term = jnp.zeros((HALF, 2 * HD), jnp.float32)
    for step in range(N_X):
        source = lax.rem(x - step + N_X, N_X)
        for flip in range(2):
            block = source * 2 + (zll + flip) % 2
            grad = jnp.concatenate([grads[step][2 * flip], grads[step][2 * flip + 1]], axis=1)
            mixed = jnp.concatenate([mine_ref[block], other_ref[block]], axis=0)
            term = term + jnp.dot(grad, mixed, preferred_element_type=jnp.float32)
    term = term.astype(jnp.bfloat16).reshape(N_YZ, ROWS, 2 * HD)
    for half in range(2):
        out_ref[:, half] = term[:, :, half * HD : (half + 1) * HD]


def weight_term(place, grads, mine, other):
    return pl.pallas_call(
        term_kernel,
        out_shape=jax.ShapeDtypeStruct((N_YZ, 2, ROWS, HD), jnp.bfloat16),
        in_specs=[pl.BlockSpec(memory_space=pltpu.SMEM)] + vmem_specs(N_X + 2),
        out_specs=vmem_specs(1)[0],
        name="weight_term",
        compiler_params=params(24),
        cost_estimate=pl.CostEstimate(
            flops=2 * HALF * 2 * N_GROUP * TOK * 2 * HD, bytes_accessed=3 << 20, transcendentals=0
        ),
    )(place, *grads, mine, other)


def total_kernel(terms_ref, out_ref):
    total = jnp.sum(terms_ref[...].astype(jnp.float32), axis=0).astype(jnp.bfloat16)
    out_ref[...] = jnp.broadcast_to(total[None], out_ref.shape)


def total(terms):
    return pl.pallas_call(
        total_kernel,
        out_shape=jax.ShapeDtypeStruct((N_REP, D_WIN // N_SHARD, HD), jnp.bfloat16),
        in_specs=vmem_specs(1),
        out_specs=vmem_specs(1)[0],
        name="total",
        compiler_params=params(8),
    )(terms)


def assemble_kernel(parts_ref, out_ref):
    for x in range(4):
        for zlh in range(2):
            for zll in range(2):
                head = (x * 2 + zll) * 2 + zlh
                part = parts_ref[x * 4 + zlh * 2 + zll]
                out_ref[:, head * HD : (head + 1) * HD] = part.astype(jnp.float32)


def assemble(parts):
    return pl.pallas_call(
        assemble_kernel,
        out_shape=jax.ShapeDtypeStruct((D_WIN // N_SHARD, HEADS * HD), jnp.float32),
        in_specs=vmem_specs(1),
        out_specs=vmem_specs(1)[0],
        name="assemble",
        compiler_params=params(8),
    )(parts)


def step(queries, keys, values, segments, grad_output):
    core = lax.axis_index("core").astype(jnp.int32)
    index = lax.axis_index("yz").astype(jnp.int32) * 2 + core
    place = jnp.stack([lax.axis_index("x"), lax.axis_index("zll")]).astype(jnp.int32)
    pay, keep, send = pack(core.reshape(1), keys, values, segments, grad_output)

    def back(steps):
        return [(s, s + steps(s)) for s in range(N_SHARD) if s + steps(s) < N_SHARD]

    def swap(value, axis):
        return lax.ppermute(value, axis, [(0, 1), (1, 0)])

    two = lax.ppermute(pay, SHARD, back(lambda s: 2))
    four = lax.ppermute(pay, SHARD, back(lambda s: 4))
    near = lax.ppermute(pay, SHARD, back(lambda s: 3 if s % 2 else 1))
    pair = jnp.stack([keep, swap(send, "core")])
    quad = jnp.concatenate([pair, swap(pair, "zll")])
    cross = swap(two, "core")
    grads = [quad]
    for step in range(1, N_X):
        around = [(s, (s + step) % N_X) for s in range(N_X)]
        grads.append(lax.ppermute(quad, "x", around))
    attention, heads = attend(index.reshape(1), queries, [pay, two, four, near, cross])
    mine = lax.all_to_all(heads, GROUP, 0, 0, tiled=True)
    term = weight_term(place, grads, mine, swap(mine, "core"))
    terms = lax.all_to_all(term.reshape(N_REST, ROWS, HD), REST, 0, 0, tiled=True)
    parts = lax.all_to_all(total(terms), REP, 0, 0, tiled=True)
    return attention, assemble(parts)


def solution(mesh):
    fine = Mesh(np.asarray(mesh.devices).reshape(SIZES), AXES)
    row = P(REP, SHARD, None)
    return jax.shard_map(
        step,
        mesh=fine,
        in_specs=(row, row, row, P(REP, SHARD), row),
        out_specs=(row, P(SHARD, None)),
        check_vma=False,
    )
```

```python
import jax
import jax.numpy as jnp
import numpy as np
from jax import lax
from jax.experimental import pallas as pl
from jax.experimental.pallas import tpu as pltpu
from jax.sharding import Mesh
from jax.sharding import PartitionSpec as P


HEADS = 16
KVH = 2
HD = 128
TOK = 128
D_WIN = 1024
SPAN = 4
N_SHARD = 32
N_REP = 16
KV = KVH * HD
PAY_ROWS = TOK + 8
NEG = -1e30
EXP2_SCALE = (HD**-0.5) * 1.4426950408889634

AXES = ("x", "zl", "yz", "core")
SIZES = (4, 4, 16, 2)
REP = ("x", "zl")
SHARD = ("yz", "core")
REST = ("yz", "zl")
N_X = 4
N_ZL = 4
N_YZ = 16
N_REST = 64
ROWS = D_WIN // N_SHARD
HALF = D_WIN // 2
WIDE = HEADS * HD // N_X
STACK = 4


def params(mib):
    return pltpu.CompilerParams(vmem_limit_bytes=mib << 20)


def vmem_specs(count):
    return [pl.BlockSpec(memory_space=pltpu.VMEM)] * count


def pack_kernel(key_ref, value_ref, seg_ref, grad_ref, pay_ref, grad_t_ref):
    pay_ref[:TOK, :KV] = key_ref[0]
    pay_ref[:TOK, KV:] = value_ref[0]
    seg = jnp.broadcast_to(seg_ref[...].astype(jnp.float32), (8, TOK))
    pay_ref[TOK:, :TOK] = seg.astype(jnp.bfloat16)
    pay_ref[TOK:, TOK:] = jnp.zeros((8, 2 * KV - TOK), jnp.bfloat16)
    grad_t = jnp.transpose(grad_ref[0].astype(jnp.float32)).reshape(N_YZ, 2, ROWS, TOK)
    for core in range(2):
        grad_t_ref[core] = grad_t[:, core].reshape(HALF, TOK).astype(jnp.bfloat16)


def pack(keys, values, segments, grad_output):
    return pl.pallas_call(
        pack_kernel,
        out_shape=(
            jax.ShapeDtypeStruct((PAY_ROWS, 2 * KV), jnp.bfloat16),
            jax.ShapeDtypeStruct((2, HALF, TOK), jnp.bfloat16),
        ),
        in_specs=vmem_specs(4),
        out_specs=tuple(vmem_specs(2)),
        name="pack",
        cost_estimate=pl.CostEstimate(flops=0, bytes_accessed=1 << 20, transcendentals=0),
    )(keys, values, segments, grad_output)


def pick_kernel(place_ref, *refs):
    other = 1 - place_ref[1]
    for step in range(N_X):
        refs[N_X][step] = refs[step][other]


def pick(place, grads):
    return pl.pallas_call(
        pick_kernel,
        out_shape=jax.ShapeDtypeStruct((N_X, HALF, TOK), jnp.bfloat16),
        in_specs=[pl.BlockSpec(memory_space=pltpu.SMEM)] + vmem_specs(N_X),
        out_specs=vmem_specs(1)[0],
        name="pick",
        compiler_params=params(8),
        cost_estimate=pl.CostEstimate(flops=0, bytes_accessed=1 << 20, transcendentals=0),
    )(place, *grads)


def attend_kernel(index_ref, query_ref, *refs):
    pays, (out_ref, swap_ref, bias_ref) = refs[: SPAN + 1], refs[SPAN + 1 :]
    index = index_ref[0]
    own_row = jnp.broadcast_to(pays[0][TOK : TOK + 1, :TOK].astype(jnp.float32), (TOK, TOK))
    q_seg = jnp.transpose(own_row)
    q_at = lax.broadcasted_iota(jnp.int32, (TOK, TOK), 0)
    k_at = lax.broadcasted_iota(jnp.int32, (TOK, TOK), 1)
    for step in range(SPAN + 1):
        k_seg = jnp.broadcast_to(pays[step][TOK : TOK + 1, :TOK].astype(jnp.float32), (TOK, TOK))
        allowed = q_seg == k_seg
        if step == 0:
            allowed = allowed & (k_at <= q_at)
        else:
            odd = lax.rem(index, 2)
            back = (0, 2, 4, 3 - 2 * odd, 1 + 2 * odd)[step]
            allowed = allowed & (k_at + (index - back) * TOK >= 0)
        bias_ref[:, step * TOK : (step + 1) * TOK] = jnp.where(allowed, 0.0, NEG)
    ones = jnp.ones((TOK, HD), jnp.bfloat16)
    for first in range(0, HEADS, STACK):
        kv_head = first // (HEADS // KVH)
        k_cols = slice(kv_head * HD, (kv_head + 1) * HD)
        v_cols = slice(KV + kv_head * HD, KV + (kv_head + 1) * HD)
        query = jnp.concatenate(
            [query_ref[0, :, h * HD : (h + 1) * HD] for h in range(first, first + STACK)], axis=0
        )
        key = jnp.concatenate([pay[:TOK, k_cols] for pay in pays], axis=0)
        scores = lax.dot_general(
            query, key, (((1,), (1,)), ((), ())), preferred_element_type=jnp.float32
        )
        bias = bias_ref[...]
        scores = scores.reshape(STACK, TOK, (SPAN + 1) * TOK) + bias[None]
        largest = jnp.max(scores, axis=-1, keepdims=True)
        weights = jnp.exp2((scores - largest) * EXP2_SCALE).astype(jnp.bfloat16)
        weights = weights.reshape(STACK * TOK, (SPAN + 1) * TOK)
        value = jnp.concatenate(
            [jnp.concatenate([pay[:TOK, v_cols], ones], axis=1) for pay in pays], axis=0
        )
        mixed = jnp.dot(weights, value, preferred_element_type=jnp.float32)
        result = (mixed[:, :HD] / mixed[:, HD:]).astype(jnp.bfloat16)
        for h in range(STACK):
            head = first + h
            rows = result[h * TOK : (h + 1) * TOK]
            out_ref[0, :, head * HD : (head + 1) * HD] = rows
            swap_ref[first // STACK, :, h * HD : (h + 1) * HD] = rows


def attend(index, queries, pays):
    return pl.pallas_call(
        attend_kernel,
        out_shape=(
            jax.ShapeDtypeStruct((1, TOK, HEADS * HD), jnp.bfloat16),
            jax.ShapeDtypeStruct((N_X, TOK, WIDE), jnp.bfloat16),
        ),
        in_specs=[pl.BlockSpec(memory_space=pltpu.SMEM)] + vmem_specs(SPAN + 2),
        out_specs=tuple(vmem_specs(2)),
        scratch_shapes=[pltpu.VMEM((TOK, (SPAN + 1) * TOK), jnp.float32)],
        name="attend",
        compiler_params=params(32),
        cost_estimate=pl.CostEstimate(
            flops=700_000_000, bytes_accessed=3 << 20, transcendentals=1_310_720
        ),
    )(index, queries, *pays)


def term_kernel(place_ref, *refs):
    grads, (far_ref, mine_ref, other_ref, out_ref) = refs[:N_X], refs[N_X:]
    x, core = place_ref[0], place_ref[1]
    term = jnp.zeros((HALF, WIDE), jnp.float32)
    for step in range(N_X):
        source = lax.rem(x - step + N_X, N_X)
        grad = jnp.concatenate([grads[step][core], far_ref[step]], axis=1)
        mixed = jnp.concatenate([mine_ref[source], other_ref[source]], axis=0)
        term = term + jnp.dot(grad, mixed, preferred_element_type=jnp.float32)
    term = term.astype(jnp.bfloat16).reshape(N_YZ, ROWS, WIDE)
    for head in range(N_ZL):
        out_ref[:, head] = term[:, :, head * HD : (head + 1) * HD]


def weight_term(place, grads, far, mine, other):
    return pl.pallas_call(
        term_kernel,
        out_shape=jax.ShapeDtypeStruct((N_YZ, N_ZL, ROWS, HD), jnp.bfloat16),
        in_specs=[pl.BlockSpec(memory_space=pltpu.SMEM)] + vmem_specs(N_X + 3),
        out_specs=vmem_specs(1)[0],
        name="weight_term",
        compiler_params=params(24),
        cost_estimate=pl.CostEstimate(
            flops=2 * HALF * 2 * N_X * TOK * WIDE, bytes_accessed=3 << 20, transcendentals=0
        ),
    )(place, *grads, far, mine, other)


def total_kernel(terms_ref, out_ref):
    total = jnp.sum(terms_ref[...].astype(jnp.float32), axis=0).astype(jnp.bfloat16)
    out_ref[...] = jnp.broadcast_to(total[None], out_ref.shape)


def total(terms):
    return pl.pallas_call(
        total_kernel,
        out_shape=jax.ShapeDtypeStruct((N_REP, D_WIN // N_SHARD, HD), jnp.bfloat16),
        in_specs=vmem_specs(1),
        out_specs=vmem_specs(1)[0],
        name="total",
        compiler_params=params(8),
    )(terms)


def assemble_kernel(parts_ref, out_ref):
    for head in range(HEADS):
        out_ref[:, head * HD : (head + 1) * HD] = parts_ref[head].astype(jnp.float32)


def assemble(parts):
    return pl.pallas_call(
        assemble_kernel,
        out_shape=jax.ShapeDtypeStruct((D_WIN // N_SHARD, HEADS * HD), jnp.float32),
        in_specs=vmem_specs(1),
        out_specs=vmem_specs(1)[0],
        name="assemble",
        compiler_params=params(8),
    )(parts)


def step(queries, keys, values, segments, grad_output):
    core = lax.axis_index("core").astype(jnp.int32)
    index = lax.axis_index("yz").astype(jnp.int32) * 2 + core
    place = jnp.stack([lax.axis_index("x").astype(jnp.int32), core])
    pay, grad_t = pack(keys, values, segments, grad_output)

    def back(steps):
        return [(s, s + steps(s)) for s in range(N_SHARD) if s + steps(s) < N_SHARD]

    def swap(value):
        return lax.ppermute(value, "core", [(0, 1), (1, 0)])

    two = lax.ppermute(pay, SHARD, back(lambda s: 2))
    four = lax.ppermute(pay, SHARD, back(lambda s: 4))
    near = lax.ppermute(pay, SHARD, back(lambda s: 3 if s % 2 else 1))
    grads = [grad_t]
    for step in range(1, N_X):
        around = [(s, (s + step) % N_X) for s in range(N_X)]
        grads.append(lax.ppermute(grad_t, "x", around))
    cross = swap(two)
    far = swap(pick(place, grads))
    attention, heads = attend(index.reshape(1), queries, [pay, two, four, near, cross])
    mine = lax.all_to_all(heads, "x", 0, 0, tiled=True)
    term = weight_term(place, grads, far, mine, swap(mine))
    terms = lax.all_to_all(term.reshape(N_REST, ROWS, HD), REST, 0, 0, tiled=True)
    parts = lax.all_to_all(total(terms), REP, 0, 0, tiled=True)
    return attention, assemble(parts)


def solution(mesh):
    fine = Mesh(np.asarray(mesh.devices).reshape(SIZES), AXES)
    row = P(REP, SHARD, None)
    return jax.shard_map(
        step,
        mesh=fine,
        in_specs=(row, row, row, P(REP, SHARD), row),
        out_specs=(row, P(SHARD, None)),
        check_vma=False,
    )
```

```python
import jax
import jax.numpy as jnp
import numpy as np
from jax import lax
from jax.experimental import pallas as pl
from jax.experimental.pallas import tpu as pltpu
from jax.sharding import Mesh
from jax.sharding import PartitionSpec as P


HEADS = 16
KVH = 2
HD = 128
TOK = 128
D_WIN = 1024
SPAN = 4
N_SHARD = 32
N_REP = 16
KV = KVH * HD
PAY_ROWS = TOK + 8
NEG = -1e30
EXP2_SCALE = (HD**-0.5) * 1.4426950408889634

AXES = ("x", "zl", "yz", "core")
SIZES = (4, 4, 16, 2)
REP = ("x", "zl")
SHARD = ("yz", "core")
GROUP = ("x", "core")
REST = ("yz", "core", "zl")
N_X = 4
N_ZL = 4
N_YZ = 16
N_GROUP = 8
ROWS = D_WIN // N_SHARD
PART = ROWS // 2
WIDE = HEADS * HD // N_GROUP
STACK = 4


def params(mib):
    return pltpu.CompilerParams(vmem_limit_bytes=mib << 20)


def vmem_specs(count):
    return [pl.BlockSpec(memory_space=pltpu.VMEM)] * count


def pack_kernel(key_ref, value_ref, seg_ref, grad_ref, pay_ref, grad_t_ref):
    pay_ref[:TOK, :KV] = key_ref[0]
    pay_ref[:TOK, KV:] = value_ref[0]
    seg = jnp.broadcast_to(seg_ref[...].astype(jnp.float32), (8, TOK))
    pay_ref[TOK:, :TOK] = seg.astype(jnp.bfloat16)
    pay_ref[TOK:, TOK:] = jnp.zeros((8, 2 * KV - TOK), jnp.bfloat16)
    grad_t = jnp.transpose(grad_ref[0].astype(jnp.float32)).astype(jnp.bfloat16)
    for x in range(N_X):
        grad_t_ref[x] = grad_t


def pack(keys, values, segments, grad_output):
    return pl.pallas_call(
        pack_kernel,
        out_shape=(
            jax.ShapeDtypeStruct((PAY_ROWS, 2 * KV), jnp.bfloat16),
            jax.ShapeDtypeStruct((N_X, D_WIN, TOK), jnp.bfloat16),
        ),
        in_specs=vmem_specs(4),
        out_specs=tuple(vmem_specs(2)),
        name="pack",
        cost_estimate=pl.CostEstimate(flops=0, bytes_accessed=1 << 20, transcendentals=0),
    )(keys, values, segments, grad_output)


def attend_kernel(index_ref, query_ref, *refs):
    pays, (out_ref, swap_ref, bias_ref) = refs[: SPAN + 1], refs[SPAN + 1 :]
    index = index_ref[0]
    own_row = jnp.broadcast_to(pays[0][TOK : TOK + 1, :TOK].astype(jnp.float32), (TOK, TOK))
    q_seg = jnp.transpose(own_row)
    q_at = lax.broadcasted_iota(jnp.int32, (TOK, TOK), 0)
    k_at = lax.broadcasted_iota(jnp.int32, (TOK, TOK), 1)
    for step in range(SPAN + 1):
        k_seg = jnp.broadcast_to(pays[step][TOK : TOK + 1, :TOK].astype(jnp.float32), (TOK, TOK))
        allowed = q_seg == k_seg
        if step == 0:
            allowed = allowed & (k_at <= q_at)
        else:
            odd = lax.rem(index, 2)
            back = (0, 2, 4, 3 - 2 * odd, 1 + 2 * odd)[step]
            allowed = allowed & (k_at + (index - back) * TOK >= 0)
        bias_ref[:, step * TOK : (step + 1) * TOK] = jnp.where(allowed, 0.0, NEG)
    ones = jnp.ones((TOK, HD), jnp.bfloat16)
    for first in range(0, HEADS, STACK):
        kv_head = first // (HEADS // KVH)
        k_cols = slice(kv_head * HD, (kv_head + 1) * HD)
        v_cols = slice(KV + kv_head * HD, KV + (kv_head + 1) * HD)
        query = jnp.concatenate(
            [query_ref[0, :, h * HD : (h + 1) * HD] for h in range(first, first + STACK)], axis=0
        )
        key = jnp.concatenate([pay[:TOK, k_cols] for pay in pays], axis=0)
        scores = lax.dot_general(
            query, key, (((1,), (1,)), ((), ())), preferred_element_type=jnp.float32
        )
        bias = bias_ref[...]
        scores = scores.reshape(STACK, TOK, (SPAN + 1) * TOK) + bias[None]
        largest = jnp.max(scores, axis=-1, keepdims=True)
        weights = jnp.exp2((scores - largest) * EXP2_SCALE).astype(jnp.bfloat16)
        weights = weights.reshape(STACK * TOK, (SPAN + 1) * TOK)
        value = jnp.concatenate(
            [jnp.concatenate([pay[:TOK, v_cols], ones], axis=1) for pay in pays], axis=0
        )
        mixed = jnp.dot(weights, value, preferred_element_type=jnp.float32)
        result = (mixed[:, :HD] / mixed[:, HD:]).astype(jnp.bfloat16)
        for h in range(STACK):
            head = first + h
            rows = result[h * TOK : (h + 1) * TOK]
            out_ref[0, :, head * HD : (head + 1) * HD] = rows
            swap_ref[head // 2, :, (head % 2) * HD : (head % 2 + 1) * HD] = rows


def attend(index, queries, pays):
    return pl.pallas_call(
        attend_kernel,
        out_shape=(
            jax.ShapeDtypeStruct((1, TOK, HEADS * HD), jnp.bfloat16),
            jax.ShapeDtypeStruct((N_GROUP, TOK, WIDE), jnp.bfloat16),
        ),
        in_specs=[pl.BlockSpec(memory_space=pltpu.SMEM)] + vmem_specs(SPAN + 2),
        out_specs=tuple(vmem_specs(2)),
        scratch_shapes=[pltpu.VMEM((TOK, (SPAN + 1) * TOK), jnp.float32)],
        name="attend",
        compiler_params=params(32),
        cost_estimate=pl.CostEstimate(
            flops=700_000_000, bytes_accessed=3 << 20, transcendentals=1_310_720
        ),
    )(index, queries, *pays)


def term_kernel(core_ref, near_ref, far_ref, mixed_ref, out_ref):
    core = core_ref[0]
    term = jnp.zeros((D_WIN, WIDE), jnp.float32)
    for x in range(N_X):
        grad = jnp.concatenate([near_ref[x], far_ref[x]], axis=1)
        mixed = jnp.concatenate([mixed_ref[2 * x + core], mixed_ref[2 * x + 1 - core]], axis=0)
        term = term + jnp.dot(grad, mixed, preferred_element_type=jnp.float32)
    term = term.astype(jnp.bfloat16).reshape(N_SHARD, 2, PART, WIDE)
    for part in range(2):
        for head in range(2):
            out_ref[:, 2 * part + head] = term[:, part, :, head * HD : (head + 1) * HD]


def weight_term(core, near, far, mixed):
    return pl.pallas_call(
        term_kernel,
        out_shape=jax.ShapeDtypeStruct((N_SHARD, N_ZL, PART, HD), jnp.bfloat16),
        in_specs=[pl.BlockSpec(memory_space=pltpu.SMEM)] + vmem_specs(3),
        out_specs=vmem_specs(1)[0],
        name="weight_term",
        compiler_params=params(24),
        cost_estimate=pl.CostEstimate(
            flops=2 * D_WIN * N_GROUP * TOK * WIDE, bytes_accessed=3 << 20, transcendentals=0
        ),
    )(core, near, far, mixed)


def total_kernel(terms_ref, out_ref):
    terms = terms_ref[...].reshape(N_YZ, 2, N_ZL, PART, HD)
    for core in range(2):
        own = terms[:, core].reshape(N_YZ * N_ZL, PART, HD).astype(jnp.float32)
        total = jnp.sum(own, axis=0).astype(jnp.bfloat16)
        out_ref[:, core] = jnp.broadcast_to(total[None], (N_REP, PART, HD))


def total(terms):
    return pl.pallas_call(
        total_kernel,
        out_shape=jax.ShapeDtypeStruct((N_REP, 2, PART, HD), jnp.bfloat16),
        in_specs=vmem_specs(1),
        out_specs=vmem_specs(1)[0],
        name="total",
        compiler_params=params(8),
    )(terms)


def assemble_kernel(parts_ref, out_ref):
    for x in range(N_X):
        for part in range(2):
            for half in range(2):
                for core in range(2):
                    head = 4 * x + 2 * core + half
                    piece = parts_ref[4 * x + 2 * part + half, core].astype(jnp.float32)
                    rows = slice(part * PART, (part + 1) * PART)
                    out_ref[rows, head * HD : (head + 1) * HD] = piece


def assemble(parts):
    return pl.pallas_call(
        assemble_kernel,
        out_shape=jax.ShapeDtypeStruct((D_WIN // N_SHARD, HEADS * HD), jnp.float32),
        in_specs=vmem_specs(1),
        out_specs=vmem_specs(1)[0],
        name="assemble",
        compiler_params=params(8),
    )(parts)


def step(queries, keys, values, segments, grad_output):
    core = lax.axis_index("core").astype(jnp.int32)
    index = lax.axis_index("yz").astype(jnp.int32) * 2 + core
    pay, grad_t = pack(keys, values, segments, grad_output)

    def back(steps):
        return [(s, s + steps(s)) for s in range(N_SHARD) if s + steps(s) < N_SHARD]

    def swap(value):
        return lax.ppermute(value, "core", [(0, 1), (1, 0)])

    two = lax.ppermute(pay, SHARD, back(lambda s: 2))
    near_grads = lax.all_to_all(grad_t, "x", 0, 0, tiled=True)
    near = lax.ppermute(pay, SHARD, back(lambda s: 3 if s % 2 else 1))
    four = lax.ppermute(pay, SHARD, back(lambda s: 4))
    cross = swap(two)
    attention, heads = attend(index.reshape(1), queries, [pay, two, four, near, cross])
    far_grads = swap(near_grads)
    mixed = lax.all_to_all(heads, GROUP, 0, 0, tiled=True)
    term = weight_term(core.reshape(1), near_grads, far_grads, mixed)
    terms = lax.all_to_all(
        term.reshape(N_SHARD * N_ZL, PART, HD), REST, 0, 0, tiled=True
    )
    parts = lax.all_to_all(total(terms), REP, 0, 0, tiled=True)
    return attention, assemble(parts)


def solution(mesh):
    fine = Mesh(np.asarray(mesh.devices).reshape(SIZES), AXES)
    row = P(REP, SHARD, None)
    return jax.shard_map(
        step,
        mesh=fine,
        in_specs=(row, row, row, P(REP, SHARD), row),
        out_specs=(row, P(SHARD, None)),
        check_vma=False,
    )
```

```python
import jax
import jax.numpy as jnp
import numpy as np
from jax import lax
from jax.experimental import pallas as pl
from jax.experimental.pallas import tpu as pltpu
from jax.sharding import Mesh
from jax.sharding import PartitionSpec as P


HEADS = 16
KVH = 2
HD = 128
TOK = 128
D_WIN = 1024
SPAN = 4
N_SHARD = 32
N_REP = 16
KV = KVH * HD
PAY_ROWS = TOK + 8
NEG = -1e30
EXP2_SCALE = (HD**-0.5) * 1.4426950408889634

AXES = ("x", "zl", "yz", "core")
SIZES = (4, 4, 16, 2)
REP = ("x", "zl")
SHARD = ("yz", "core")
GROUP = ("x", "core")
REST = ("yz", "zl")
N_X = 4
N_ZL = 4
N_YZ = 16
N_GROUP = 8
N_REST = 64
ROWS = D_WIN // N_SHARD
HALF = D_WIN // 2
WIDE = HEADS * HD // N_X
STACK = 4


def params(mib):
    return pltpu.CompilerParams(vmem_limit_bytes=mib << 20)


def vmem_specs(count):
    return [pl.BlockSpec(memory_space=pltpu.VMEM)] * count


def pack_kernel(key_ref, value_ref, seg_ref, grad_ref, pay_ref, grad_t_ref):
    pay_ref[:TOK, :KV] = key_ref[0]
    pay_ref[:TOK, KV:] = value_ref[0]
    seg = jnp.broadcast_to(seg_ref[...].astype(jnp.float32), (8, TOK))
    pay_ref[TOK:, :TOK] = seg.astype(jnp.bfloat16)
    pay_ref[TOK:, TOK:] = jnp.zeros((8, 2 * KV - TOK), jnp.bfloat16)
    grad_t = jnp.transpose(grad_ref[0].astype(jnp.float32)).reshape(N_YZ, 2, ROWS, TOK)
    for core in range(2):
        rows = grad_t[:, core].reshape(HALF, TOK).astype(jnp.bfloat16)
        for x in range(N_X):
            grad_t_ref[2 * x + core] = rows


def pack(keys, values, segments, grad_output):
    return pl.pallas_call(
        pack_kernel,
        out_shape=(
            jax.ShapeDtypeStruct((PAY_ROWS, 2 * KV), jnp.bfloat16),
            jax.ShapeDtypeStruct((N_GROUP, HALF, TOK), jnp.bfloat16),
        ),
        in_specs=vmem_specs(4),
        out_specs=tuple(vmem_specs(2)),
        name="pack",
        cost_estimate=pl.CostEstimate(flops=0, bytes_accessed=1 << 20, transcendentals=0),
    )(keys, values, segments, grad_output)


def attend_kernel(index_ref, query_ref, *refs):
    pays, (out_ref, swap_ref, bias_ref) = refs[: SPAN + 1], refs[SPAN + 1 :]
    index = index_ref[0]
    own_row = jnp.broadcast_to(pays[0][TOK : TOK + 1, :TOK].astype(jnp.float32), (TOK, TOK))
    q_seg = jnp.transpose(own_row)
    q_at = lax.broadcasted_iota(jnp.int32, (TOK, TOK), 0)
    k_at = lax.broadcasted_iota(jnp.int32, (TOK, TOK), 1)
    for step in range(SPAN + 1):
        k_seg = jnp.broadcast_to(pays[step][TOK : TOK + 1, :TOK].astype(jnp.float32), (TOK, TOK))
        allowed = q_seg == k_seg
        if step == 0:
            allowed = allowed & (k_at <= q_at)
        else:
            odd = lax.rem(index, 2)
            back = (0, 2, 4, 3 - 2 * odd, 1 + 2 * odd)[step]
            allowed = allowed & (k_at + (index - back) * TOK >= 0)
        bias_ref[:, step * TOK : (step + 1) * TOK] = jnp.where(allowed, 0.0, NEG)
    ones = jnp.ones((TOK, HD), jnp.bfloat16)
    for first in range(0, HEADS, STACK):
        kv_head = first // (HEADS // KVH)
        k_cols = slice(kv_head * HD, (kv_head + 1) * HD)
        v_cols = slice(KV + kv_head * HD, KV + (kv_head + 1) * HD)
        query = jnp.concatenate(
            [query_ref[0, :, h * HD : (h + 1) * HD] for h in range(first, first + STACK)], axis=0
        )
        key = jnp.concatenate([pay[:TOK, k_cols] for pay in pays], axis=0)
        scores = lax.dot_general(
            query, key, (((1,), (1,)), ((), ())), preferred_element_type=jnp.float32
        )
        bias = bias_ref[...]
        scores = scores.reshape(STACK, TOK, (SPAN + 1) * TOK) + bias[None]
        largest = jnp.max(scores, axis=-1, keepdims=True)
        weights = jnp.exp2((scores - largest) * EXP2_SCALE).astype(jnp.bfloat16)
        weights = weights.reshape(STACK * TOK, (SPAN + 1) * TOK)
        value = jnp.concatenate(
            [jnp.concatenate([pay[:TOK, v_cols], ones], axis=1) for pay in pays], axis=0
        )
        mixed = jnp.dot(weights, value, preferred_element_type=jnp.float32)
        result = (mixed[:, :HD] / mixed[:, HD:]).astype(jnp.bfloat16)
        for h in range(STACK):
            head = first + h
            rows = result[h * TOK : (h + 1) * TOK]
            out_ref[0, :, head * HD : (head + 1) * HD] = rows
            swap_ref[first // STACK, :, h * HD : (h + 1) * HD] = rows


def attend(index, queries, pays):
    return pl.pallas_call(
        attend_kernel,
        out_shape=(
            jax.ShapeDtypeStruct((1, TOK, HEADS * HD), jnp.bfloat16),
            jax.ShapeDtypeStruct((N_X, TOK, WIDE), jnp.bfloat16),
        ),
        in_specs=[pl.BlockSpec(memory_space=pltpu.SMEM)] + vmem_specs(SPAN + 2),
        out_specs=tuple(vmem_specs(2)),
        scratch_shapes=[pltpu.VMEM((TOK, (SPAN + 1) * TOK), jnp.float32)],
        name="attend",
        compiler_params=params(32),
        cost_estimate=pl.CostEstimate(
            flops=700_000_000, bytes_accessed=3 << 20, transcendentals=1_310_720
        ),
    )(index, queries, *pays)


def term_kernel(core_ref, grads_ref, mine_ref, other_ref, out_ref):
    core = core_ref[0]
    term = jnp.zeros((HALF, WIDE), jnp.float32)
    for x in range(N_X):
        grad = jnp.concatenate([grads_ref[2 * x + core], grads_ref[2 * x + 1 - core]], axis=1)
        mixed = jnp.concatenate([mine_ref[x], other_ref[x]], axis=0)
        term = term + jnp.dot(grad, mixed, preferred_element_type=jnp.float32)
    term = term.astype(jnp.bfloat16).reshape(N_YZ, ROWS, WIDE)
    for head in range(N_ZL):
        out_ref[:, head] = term[:, :, head * HD : (head + 1) * HD]


def weight_term(core, grads, mine, other):
    return pl.pallas_call(
        term_kernel,
        out_shape=jax.ShapeDtypeStruct((N_YZ, N_ZL, ROWS, HD), jnp.bfloat16),
        in_specs=[pl.BlockSpec(memory_space=pltpu.SMEM)] + vmem_specs(3),
        out_specs=vmem_specs(1)[0],
        name="weight_term",
        compiler_params=params(24),
        cost_estimate=pl.CostEstimate(
            flops=2 * HALF * N_GROUP * TOK * WIDE, bytes_accessed=3 << 20, transcendentals=0
        ),
    )(core, grads, mine, other)


def total_kernel(terms_ref, out_ref):
    total = jnp.sum(terms_ref[...].astype(jnp.float32), axis=0).astype(jnp.bfloat16)
    out_ref[...] = jnp.broadcast_to(total[None], out_ref.shape)


def total(terms):
    return pl.pallas_call(
        total_kernel,
        out_shape=jax.ShapeDtypeStruct((N_REP, D_WIN // N_SHARD, HD), jnp.bfloat16),
        in_specs=vmem_specs(1),
        out_specs=vmem_specs(1)[0],
        name="total",
        compiler_params=params(8),
    )(terms)


def assemble_kernel(parts_ref, out_ref):
    for head in range(HEADS):
        out_ref[:, head * HD : (head + 1) * HD] = parts_ref[head].astype(jnp.float32)


def assemble(parts):
    return pl.pallas_call(
        assemble_kernel,
        out_shape=jax.ShapeDtypeStruct((D_WIN // N_SHARD, HEADS * HD), jnp.float32),
        in_specs=vmem_specs(1),
        out_specs=vmem_specs(1)[0],
        name="assemble",
        compiler_params=params(8),
    )(parts)


def step(queries, keys, values, segments, grad_output):
    core = lax.axis_index("core").astype(jnp.int32)
    index = lax.axis_index("yz").astype(jnp.int32) * 2 + core
    pay, grad_t = pack(keys, values, segments, grad_output)

    def back(steps):
        return [(s, s + steps(s)) for s in range(N_SHARD) if s + steps(s) < N_SHARD]

    def swap(value):
        return lax.ppermute(value, "core", [(0, 1), (1, 0)])

    two = lax.ppermute(pay, SHARD, back(lambda s: 2))
    grads = lax.all_to_all(grad_t, GROUP, 0, 0, tiled=True)
    near = lax.ppermute(pay, SHARD, back(lambda s: 3 if s % 2 else 1))
    four = lax.ppermute(pay, SHARD, back(lambda s: 4))
    cross = swap(two)
    attention, heads = attend(index.reshape(1), queries, [pay, two, four, near, cross])
    mine = lax.all_to_all(heads, "x", 0, 0, tiled=True)
    other = swap(mine)
    term = weight_term(core.reshape(1), grads, mine, other)
    terms = lax.all_to_all(term.reshape(N_REST, ROWS, HD), REST, 0, 0, tiled=True)
    parts = lax.all_to_all(total(terms), REP, 0, 0, tiled=True)
    return attention, assemble(parts)


def solution(mesh):
    fine = Mesh(np.asarray(mesh.devices).reshape(SIZES), AXES)
    row = P(REP, SHARD, None)
    return jax.shard_map(
        step,
        mesh=fine,
        in_specs=(row, row, row, P(REP, SHARD), row),
        out_specs=(row, P(SHARD, None)),
        check_vma=False,
    )
```

```python
import jax
import jax.numpy as jnp
import numpy as np
from jax import lax
from jax.experimental import pallas as pl
from jax.experimental.pallas import tpu as pltpu
from jax.sharding import Mesh
from jax.sharding import PartitionSpec as P


HEADS = 16
KVH = 2
HD = 128
TOK = 128
D_WIN = 1024
SPAN = 4
N_SHARD = 32
N_REP = 16
KV = KVH * HD
PAY_ROWS = TOK + 8
NEG = -1e30
EXP2_SCALE = (HD**-0.5) * 1.4426950408889634

AXES = ("x", "zl", "y", "zh", "core")
SIZES = (4, 4, 8, 2, 2)
REP = ("x", "zl")
SHARD = ("y", "zh", "core")
GROUP = ("x", "core")
REST = ("zl", "zh", "y")
N_X = 4
N_ZL = 4
N_Y = 8
N_ZH = 2
N_YZ = N_Y * N_ZH
N_GROUP = 8
N_REST = 64
ROWS = D_WIN // N_SHARD
HALF = D_WIN // 2
WIDE = HEADS * HD // N_X
STACK = 4


def params(mib):
    return pltpu.CompilerParams(vmem_limit_bytes=mib << 20)


def vmem_specs(count):
    return [pl.BlockSpec(memory_space=pltpu.VMEM)] * count


def pack_kernel(key_ref, value_ref, seg_ref, pay_ref):
    pay_ref[:TOK, :KV] = key_ref[0]
    pay_ref[:TOK, KV:] = value_ref[0]
    seg = jnp.broadcast_to(seg_ref[...].astype(jnp.float32), (8, TOK))
    pay_ref[TOK:, :TOK] = seg.astype(jnp.bfloat16)
    pay_ref[TOK:, TOK:] = jnp.zeros((8, 2 * KV - TOK), jnp.bfloat16)


def pack(keys, values, segments):
    return pl.pallas_call(
        pack_kernel,
        out_shape=jax.ShapeDtypeStruct((PAY_ROWS, 2 * KV), jnp.bfloat16),
        in_specs=vmem_specs(3),
        out_specs=vmem_specs(1)[0],
        name="pack",
        cost_estimate=pl.CostEstimate(flops=0, bytes_accessed=1 << 18, transcendentals=0),
    )(keys, values, segments)


def turn_kernel(grad_ref, grad_t_ref):
    grad_t = jnp.transpose(grad_ref[0].astype(jnp.float32)).reshape(N_YZ, 2, ROWS, TOK)
    for core in range(2):
        rows = grad_t[:, core].reshape(HALF, TOK).astype(jnp.bfloat16)
        for x in range(N_X):
            grad_t_ref[2 * x + core] = rows


def turn(grad_output):
    return pl.pallas_call(
        turn_kernel,
        out_shape=jax.ShapeDtypeStruct((N_GROUP, HALF, TOK), jnp.bfloat16),
        in_specs=vmem_specs(1),
        out_specs=vmem_specs(1)[0],
        name="turn",
        cost_estimate=pl.CostEstimate(flops=0, bytes_accessed=1 << 20, transcendentals=0),
    )(grad_output)


def attend_kernel(index_ref, query_ref, *refs):
    pays, (out_ref, swap_ref, bias_ref) = refs[: SPAN + 1], refs[SPAN + 1 :]
    index = index_ref[0]
    own_row = jnp.broadcast_to(pays[0][TOK : TOK + 1, :TOK].astype(jnp.float32), (TOK, TOK))
    q_seg = jnp.transpose(own_row)
    q_at = lax.broadcasted_iota(jnp.int32, (TOK, TOK), 0)
    k_at = lax.broadcasted_iota(jnp.int32, (TOK, TOK), 1)
    for step in range(SPAN + 1):
        k_seg = jnp.broadcast_to(pays[step][TOK : TOK + 1, :TOK].astype(jnp.float32), (TOK, TOK))
        allowed = q_seg == k_seg
        if step == 0:
            allowed = allowed & (k_at <= q_at)
        else:
            odd = lax.rem(index, 2)
            back = (0, 2, 4, 3 - 2 * odd, 1 + 2 * odd)[step]
            allowed = allowed & (k_at + (index - back) * TOK >= 0)
        bias_ref[:, step * TOK : (step + 1) * TOK] = jnp.where(allowed, 0.0, NEG)
    ones = jnp.ones((TOK, HD), jnp.bfloat16)
    for first in range(0, HEADS, STACK):
        kv_head = first // (HEADS // KVH)
        k_cols = slice(kv_head * HD, (kv_head + 1) * HD)
        v_cols = slice(KV + kv_head * HD, KV + (kv_head + 1) * HD)
        query = jnp.concatenate(
            [query_ref[0, :, h * HD : (h + 1) * HD] for h in range(first, first + STACK)], axis=0
        )
        key = jnp.concatenate([pay[:TOK, k_cols] for pay in pays], axis=0)
        scores = lax.dot_general(
            query, key, (((1,), (1,)), ((), ())), preferred_element_type=jnp.float32
        )
        bias = bias_ref[...]
        scores = scores.reshape(STACK, TOK, (SPAN + 1) * TOK) + bias[None]
        largest = jnp.max(scores, axis=-1, keepdims=True)
        weights = jnp.exp2((scores - largest) * EXP2_SCALE).astype(jnp.bfloat16)
        weights = weights.reshape(STACK * TOK, (SPAN + 1) * TOK)
        value = jnp.concatenate(
            [jnp.concatenate([pay[:TOK, v_cols], ones], axis=1) for pay in pays], axis=0
        )
        mixed = jnp.dot(weights, value, preferred_element_type=jnp.float32)
        result = (mixed[:, :HD] / mixed[:, HD:]).astype(jnp.bfloat16)
        for h in range(STACK):
            head = first + h
            rows = result[h * TOK : (h + 1) * TOK]
            out_ref[0, :, head * HD : (head + 1) * HD] = rows
            swap_ref[first // STACK, :, h * HD : (h + 1) * HD] = rows


def attend(index, queries, pays):
    return pl.pallas_call(
        attend_kernel,
        out_shape=(
            jax.ShapeDtypeStruct((1, TOK, HEADS * HD), jnp.bfloat16),
            jax.ShapeDtypeStruct((N_X, TOK, WIDE), jnp.bfloat16),
        ),
        in_specs=[pl.BlockSpec(memory_space=pltpu.SMEM)] + vmem_specs(SPAN + 2),
        out_specs=tuple(vmem_specs(2)),
        scratch_shapes=[pltpu.VMEM((TOK, (SPAN + 1) * TOK), jnp.float32)],
        name="attend",
        compiler_params=params(32),
        cost_estimate=pl.CostEstimate(
            flops=700_000_000, bytes_accessed=3 << 20, transcendentals=1_310_720
        ),
    )(index, queries, *pays)


def term_kernel(core_ref, grads_ref, mine_ref, other_ref, out_ref):
    core = core_ref[0]
    term = jnp.zeros((HALF, WIDE), jnp.float32)
    for x in range(N_X):
        grad = jnp.concatenate([grads_ref[2 * x + core], grads_ref[2 * x + 1 - core]], axis=1)
        mixed = jnp.concatenate([mine_ref[x], other_ref[x]], axis=0)
        term = term + jnp.dot(grad, mixed, preferred_element_type=jnp.float32)
    term = term.astype(jnp.bfloat16).reshape(N_Y, N_ZH, ROWS, WIDE)
    for head in range(N_ZL):
        for zh in range(N_ZH):
            out_ref[head, zh] = term[:, zh, :, head * HD : (head + 1) * HD]


def weight_term(core, grads, mine, other):
    return pl.pallas_call(
        term_kernel,
        out_shape=jax.ShapeDtypeStruct((N_ZL, N_ZH, N_Y, ROWS, HD), jnp.bfloat16),
        in_specs=[pl.BlockSpec(memory_space=pltpu.SMEM)] + vmem_specs(3),
        out_specs=vmem_specs(1)[0],
        name="weight_term",
        compiler_params=params(24),
        cost_estimate=pl.CostEstimate(
            flops=2 * HALF * N_GROUP * TOK * WIDE, bytes_accessed=3 << 20, transcendentals=0
        ),
    )(core, grads, mine, other)


def total_kernel(terms_ref, out_ref):
    total = jnp.sum(terms_ref[...].astype(jnp.float32), axis=0).astype(jnp.bfloat16)
    out_ref[...] = jnp.broadcast_to(total[None], out_ref.shape)


def total(terms):
    return pl.pallas_call(
        total_kernel,
        out_shape=jax.ShapeDtypeStruct((N_REP, D_WIN // N_SHARD, HD), jnp.bfloat16),
        in_specs=vmem_specs(1),
        out_specs=vmem_specs(1)[0],
        name="total",
        compiler_params=params(8),
    )(terms)


def assemble_kernel(parts_ref, out_ref):
    for head in range(HEADS):
        out_ref[:, head * HD : (head + 1) * HD] = parts_ref[head].astype(jnp.float32)


def assemble(parts):
    return pl.pallas_call(
        assemble_kernel,
        out_shape=jax.ShapeDtypeStruct((D_WIN // N_SHARD, HEADS * HD), jnp.float32),
        in_specs=vmem_specs(1),
        out_specs=vmem_specs(1)[0],
        name="assemble",
        compiler_params=params(8),
    )(parts)


def step(queries, keys, values, segments, grad_output):
    core = lax.axis_index("core").astype(jnp.int32)
    index = lax.axis_index(SHARD).astype(jnp.int32)
    pay = pack(keys, values, segments)

    def back(steps):
        return [(s, s + steps(s)) for s in range(N_SHARD) if s + steps(s) < N_SHARD]

    def swap(value):
        return lax.ppermute(value, "core", [(0, 1), (1, 0)])

    two = lax.ppermute(pay, SHARD, back(lambda s: 2))
    grads = lax.all_to_all(turn(grad_output), GROUP, 0, 0, tiled=True)
    near = lax.ppermute(pay, SHARD, back(lambda s: 3 if s % 2 else 1))
    four = lax.ppermute(pay, SHARD, back(lambda s: 4))
    cross = swap(two)
    attention, heads = attend(index.reshape(1), queries, [pay, two, four, near, cross])
    mine = lax.all_to_all(heads, "x", 0, 0, tiled=True)
    other = swap(mine)
    term = weight_term(core.reshape(1), grads, mine, other)
    terms = lax.all_to_all(term.reshape(N_REST, ROWS, HD), REST, 0, 0, tiled=True)
    parts = lax.all_to_all(total(terms), REP, 0, 0, tiled=True)
    return attention, assemble(parts)


def solution(mesh):
    fine = Mesh(np.asarray(mesh.devices).reshape(SIZES), AXES)
    row = P(REP, SHARD, None)
    return jax.shard_map(
        step,
        mesh=fine,
        in_specs=(row, row, row, P(REP, SHARD), row),
        out_specs=(row, P(SHARD, None)),
        check_vma=False,
    )
```

```python
import jax
import jax.numpy as jnp
import numpy as np
from jax import lax
from jax.experimental import pallas as pl
from jax.experimental.pallas import tpu as pltpu
from jax.sharding import Mesh
from jax.sharding import PartitionSpec as P


HEADS = 16
KVH = 2
HD = 128
TOK = 128
D_WIN = 1024
SPAN = 4
N_SHARD = 32
N_REP = 16
KV = KVH * HD
PAY_ROWS = TOK + 8
NEG = -1e30
EXP2_SCALE = (HD**-0.5) * 1.4426950408889634

AXES = ("x", "zl", "y", "zh", "core")
SIZES = (4, 4, 8, 2, 2)
REP = ("x", "zl")
SHARD = ("y", "zh", "core")
GROUP = ("x", "core")
REST = ("zl", "core", "zh", "y")
N_X = 4
N_ZL = 4
N_Y = 8
N_ZH = 2
N_YZ = N_Y * N_ZH
N_GROUP = 8
ROWS = D_WIN // N_SHARD
PART = ROWS // 2
WIDE = HEADS * HD // N_GROUP
STACK = 4


def params(mib):
    return pltpu.CompilerParams(vmem_limit_bytes=mib << 20)


def vmem_specs(count):
    return [pl.BlockSpec(memory_space=pltpu.VMEM)] * count


def pack_kernel(key_ref, value_ref, seg_ref, grad_ref, pay_ref, grad_t_ref):
    pay_ref[:TOK, :KV] = key_ref[0]
    pay_ref[:TOK, KV:] = value_ref[0]
    seg = jnp.broadcast_to(seg_ref[...].astype(jnp.float32), (8, TOK))
    pay_ref[TOK:, :TOK] = seg.astype(jnp.bfloat16)
    pay_ref[TOK:, TOK:] = jnp.zeros((8, 2 * KV - TOK), jnp.bfloat16)
    grad_t = jnp.transpose(grad_ref[0].astype(jnp.float32)).astype(jnp.bfloat16)
    for x in range(N_X):
        grad_t_ref[x] = grad_t


def pack(keys, values, segments, grad_output):
    return pl.pallas_call(
        pack_kernel,
        out_shape=(
            jax.ShapeDtypeStruct((PAY_ROWS, 2 * KV), jnp.bfloat16),
            jax.ShapeDtypeStruct((N_X, D_WIN, TOK), jnp.bfloat16),
        ),
        in_specs=vmem_specs(4),
        out_specs=tuple(vmem_specs(2)),
        name="pack",
        cost_estimate=pl.CostEstimate(flops=0, bytes_accessed=1 << 20, transcendentals=0),
    )(keys, values, segments, grad_output)


def attend_kernel(index_ref, query_ref, *refs):
    pays, (out_ref, swap_ref, bias_ref) = refs[: SPAN + 1], refs[SPAN + 1 :]
    index = index_ref[0]
    own_row = jnp.broadcast_to(pays[0][TOK : TOK + 1, :TOK].astype(jnp.float32), (TOK, TOK))
    q_seg = jnp.transpose(own_row)
    q_at = lax.broadcasted_iota(jnp.int32, (TOK, TOK), 0)
    k_at = lax.broadcasted_iota(jnp.int32, (TOK, TOK), 1)
    for step in range(SPAN + 1):
        k_seg = jnp.broadcast_to(pays[step][TOK : TOK + 1, :TOK].astype(jnp.float32), (TOK, TOK))
        allowed = q_seg == k_seg
        if step == 0:
            allowed = allowed & (k_at <= q_at)
        else:
            odd = lax.rem(index, 2)
            back = (0, 2, 4, 3 - 2 * odd, 1 + 2 * odd)[step]
            allowed = allowed & (k_at + (index - back) * TOK >= 0)
        bias_ref[:, step * TOK : (step + 1) * TOK] = jnp.where(allowed, 0.0, NEG)
    ones = jnp.ones((TOK, HD), jnp.bfloat16)
    for first in range(0, HEADS, STACK):
        kv_head = first // (HEADS // KVH)
        k_cols = slice(kv_head * HD, (kv_head + 1) * HD)
        v_cols = slice(KV + kv_head * HD, KV + (kv_head + 1) * HD)
        query = jnp.concatenate(
            [query_ref[0, :, h * HD : (h + 1) * HD] for h in range(first, first + STACK)], axis=0
        )
        key = jnp.concatenate([pay[:TOK, k_cols] for pay in pays], axis=0)
        scores = lax.dot_general(
            query, key, (((1,), (1,)), ((), ())), preferred_element_type=jnp.float32
        )
        bias = bias_ref[...]
        scores = scores.reshape(STACK, TOK, (SPAN + 1) * TOK) + bias[None]
        largest = jnp.max(scores, axis=-1, keepdims=True)
        weights = jnp.exp2((scores - largest) * EXP2_SCALE).astype(jnp.bfloat16)
        weights = weights.reshape(STACK * TOK, (SPAN + 1) * TOK)
        value = jnp.concatenate(
            [jnp.concatenate([pay[:TOK, v_cols], ones], axis=1) for pay in pays], axis=0
        )
        mixed = jnp.dot(weights, value, preferred_element_type=jnp.float32)
        result = (mixed[:, :HD] / mixed[:, HD:]).astype(jnp.bfloat16)
        for h in range(STACK):
            head = first + h
            rows = result[h * TOK : (h + 1) * TOK]
            out_ref[0, :, head * HD : (head + 1) * HD] = rows
            swap_ref[head // 2, :, (head % 2) * HD : (head % 2 + 1) * HD] = rows


def attend(index, queries, pays):
    return pl.pallas_call(
        attend_kernel,
        out_shape=(
            jax.ShapeDtypeStruct((1, TOK, HEADS * HD), jnp.bfloat16),
            jax.ShapeDtypeStruct((N_GROUP, TOK, WIDE), jnp.bfloat16),
        ),
        in_specs=[pl.BlockSpec(memory_space=pltpu.SMEM)] + vmem_specs(SPAN + 2),
        out_specs=tuple(vmem_specs(2)),
        scratch_shapes=[pltpu.VMEM((TOK, (SPAN + 1) * TOK), jnp.float32)],
        name="attend",
        compiler_params=params(32),
        cost_estimate=pl.CostEstimate(
            flops=700_000_000, bytes_accessed=3 << 20, transcendentals=1_310_720
        ),
    )(index, queries, *pays)


def term_kernel(core_ref, near_ref, far_ref, mixed_ref, out_ref):
    core = core_ref[0]
    term = jnp.zeros((D_WIN, WIDE), jnp.float32)
    for x in range(N_X):
        grad = jnp.concatenate([near_ref[x], far_ref[x]], axis=1)
        mixed = jnp.concatenate([mixed_ref[2 * x + core], mixed_ref[2 * x + 1 - core]], axis=0)
        term = term + jnp.dot(grad, mixed, preferred_element_type=jnp.float32)
    term = term.astype(jnp.bfloat16).reshape(N_Y, N_ZH, 2, 2, PART, WIDE)
    for part in range(2):
        for head in range(2):
            columns = slice(head * HD, (head + 1) * HD)
            for to_core in range(2):
                for zh in range(N_ZH):
                    out_ref[2 * part + head, to_core, zh] = term[:, zh, to_core, part, :, columns]


def weight_term(core, near, far, mixed):
    return pl.pallas_call(
        term_kernel,
        out_shape=jax.ShapeDtypeStruct((N_ZL, 2, N_ZH, N_Y, PART, HD), jnp.bfloat16),
        in_specs=[pl.BlockSpec(memory_space=pltpu.SMEM)] + vmem_specs(3),
        out_specs=vmem_specs(1)[0],
        name="weight_term",
        compiler_params=params(24),
        cost_estimate=pl.CostEstimate(
            flops=2 * D_WIN * N_GROUP * TOK * WIDE, bytes_accessed=3 << 20, transcendentals=0
        ),
    )(core, near, far, mixed)


def total_kernel(terms_ref, out_ref):
    terms = terms_ref[...].reshape(N_ZL, 2, N_YZ, PART, HD)
    for core in range(2):
        own = terms[:, core].reshape(N_ZL * N_YZ, PART, HD).astype(jnp.float32)
        total = jnp.sum(own, axis=0).astype(jnp.bfloat16)
        out_ref[:, core] = jnp.broadcast_to(total[None], (N_REP, PART, HD))


def total(terms):
    return pl.pallas_call(
        total_kernel,
        out_shape=jax.ShapeDtypeStruct((N_REP, 2, PART, HD), jnp.bfloat16),
        in_specs=vmem_specs(1),
        out_specs=vmem_specs(1)[0],
        name="total",
        compiler_params=params(8),
    )(terms)


def assemble_kernel(parts_ref, out_ref):
    for x in range(N_X):
        for part in range(2):
            for half in range(2):
                for core in range(2):
                    head = 4 * x + 2 * core + half
                    piece = parts_ref[4 * x + 2 * part + half, core].astype(jnp.float32)
                    rows = slice(part * PART, (part + 1) * PART)
                    out_ref[rows, head * HD : (head + 1) * HD] = piece


def assemble(parts):
    return pl.pallas_call(
        assemble_kernel,
        out_shape=jax.ShapeDtypeStruct((D_WIN // N_SHARD, HEADS * HD), jnp.float32),
        in_specs=vmem_specs(1),
        out_specs=vmem_specs(1)[0],
        name="assemble",
        compiler_params=params(8),
    )(parts)


def step(queries, keys, values, segments, grad_output):
    core = lax.axis_index("core").astype(jnp.int32)
    index = lax.axis_index(SHARD).astype(jnp.int32)
    pay, grad_t = pack(keys, values, segments, grad_output)

    def back(steps):
        return [(s, s + steps(s)) for s in range(N_SHARD) if s + steps(s) < N_SHARD]

    def swap(value):
        return lax.ppermute(value, "core", [(0, 1), (1, 0)])

    two = lax.ppermute(pay, SHARD, back(lambda s: 2))
    near_grads = lax.all_to_all(grad_t, "x", 0, 0, tiled=True)
    near = lax.ppermute(pay, SHARD, back(lambda s: 3 if s % 2 else 1))
    four = lax.ppermute(pay, SHARD, back(lambda s: 4))
    cross = swap(two)
    attention, heads = attend(index.reshape(1), queries, [pay, two, four, near, cross])
    far_grads = swap(near_grads)
    mixed = lax.all_to_all(heads, GROUP, 0, 0, tiled=True)
    term = weight_term(core.reshape(1), near_grads, far_grads, mixed)
    terms = lax.all_to_all(
        term.reshape(N_SHARD * N_ZL, PART, HD), REST, 0, 0, tiled=True
    )
    parts = lax.all_to_all(total(terms), REP, 0, 0, tiled=True)
    return attention, assemble(parts)


def solution(mesh):
    fine = Mesh(np.asarray(mesh.devices).reshape(SIZES), AXES)
    row = P(REP, SHARD, None)
    return jax.shard_map(
        step,
        mesh=fine,
        in_specs=(row, row, row, P(REP, SHARD), row),
        out_specs=(row, P(SHARD, None)),
        check_vma=False,
    )
```

```python
import jax
import jax.numpy as jnp
import numpy as np
from jax import lax
from jax.experimental import pallas as pl
from jax.experimental.pallas import tpu as pltpu
from jax.sharding import Mesh
from jax.sharding import PartitionSpec as P


HEADS = 16
KVH = 2
HD = 128
TOK = 128
D_WIN = 1024
SPAN = 4
N_SHARD = 32
N_REP = 16
KV = KVH * HD
PAY_ROWS = TOK + 8
NEG = -1e30
EXP2_SCALE = (HD**-0.5) * 1.4426950408889634

AXES = ("x", "zl", "y", "zh", "core")
SIZES = (4, 4, 8, 2, 2)
REP = ("x", "zl")
SHARD = ("y", "zh", "core")
GROUP = ("x", "core")
REST = ("zl", "core", "zh", "y")
N_X = 4
N_ZL = 4
N_Y = 8
N_ZH = 2
N_YZ = N_Y * N_ZH
N_GROUP = 8
ROWS = D_WIN // N_SHARD
PART = ROWS // 2
WIDE = HEADS * HD // N_GROUP
STACK = 8


def params(mib):
    return pltpu.CompilerParams(vmem_limit_bytes=mib << 20)


def vmem_specs(count):
    return [pl.BlockSpec(memory_space=pltpu.VMEM)] * count


def pack_kernel(*refs):
    sources, (pay_out, grad_t_out), held = refs[:4], refs[4:6], refs[6:10]
    pay_ref, grad_t_ref, sems = refs[10:]
    copies = [
        pltpu.make_async_copy(source, here, sems.at[i])
        for i, (source, here) in enumerate(zip(sources, held))
    ]
    for copy in copies:
        copy.start()
    key_ref, value_ref, seg_ref, grad_ref = held
    pay_ref[TOK:, TOK:] = jnp.zeros((8, 2 * KV - TOK), jnp.bfloat16)
    for copy in copies[:3]:
        copy.wait()
    pay_ref[:TOK, :KV] = key_ref[0]
    pay_ref[:TOK, KV:] = value_ref[0]
    seg = jnp.broadcast_to(seg_ref[...].astype(jnp.float32), (8, TOK))
    pay_ref[TOK:, :TOK] = seg.astype(jnp.bfloat16)
    results = [pltpu.make_async_copy(pay_ref, pay_out, sems.at[4])]
    results[0].start()
    copies[3].wait()
    grad_t_ref[...] = jnp.transpose(grad_ref[0].astype(jnp.float32)).astype(jnp.bfloat16)
    for x in range(N_X):
        results.append(pltpu.make_async_copy(grad_t_ref, grad_t_out.at[x], sems.at[5 + x]))
        results[-1].start()
    for result in results:
        result.wait()


def pack(keys, values, segments, grad_output):
    sources = (keys, values, segments, grad_output)
    anywhere = pl.BlockSpec(memory_space=pl.ANY)
    return pl.pallas_call(
        pack_kernel,
        out_shape=(
            jax.ShapeDtypeStruct((PAY_ROWS, 2 * KV), jnp.bfloat16),
            jax.ShapeDtypeStruct((N_X, D_WIN, TOK), jnp.bfloat16),
        ),
        in_specs=[anywhere] * 4,
        out_specs=(anywhere, anywhere),
        scratch_shapes=[pltpu.VMEM(source.shape, source.dtype) for source in sources]
        + [
            pltpu.VMEM((PAY_ROWS, 2 * KV), jnp.bfloat16),
            pltpu.VMEM((D_WIN, TOK), jnp.bfloat16),
            pltpu.SemaphoreType.DMA((5 + N_X,)),
        ],
        name="pack",
        cost_estimate=pl.CostEstimate(flops=0, bytes_accessed=1 << 20, transcendentals=0),
    )(*sources)


def attend_kernel(index_ref, query_ref, *refs):
    pays, (out_ref, swap_ref, bias_ref) = refs[: SPAN + 1], refs[SPAN + 1 :]
    index = index_ref[0]
    own_row = jnp.broadcast_to(pays[0][TOK : TOK + 1, :TOK].astype(jnp.float32), (TOK, TOK))
    q_seg = jnp.transpose(own_row)
    q_at = lax.broadcasted_iota(jnp.int32, (TOK, TOK), 0)
    k_at = lax.broadcasted_iota(jnp.int32, (TOK, TOK), 1)
    for step in range(SPAN + 1):
        k_seg = jnp.broadcast_to(pays[step][TOK : TOK + 1, :TOK].astype(jnp.float32), (TOK, TOK))
        allowed = q_seg == k_seg
        if step == 0:
            allowed = allowed & (k_at <= q_at)
        else:
            odd = lax.rem(index, 2)
            back = (0, 2, 4, 3 - 2 * odd, 1 + 2 * odd)[step]
            allowed = allowed & (k_at + (index - back) * TOK >= 0)
        bias_ref[:, step * TOK : (step + 1) * TOK] = jnp.where(allowed, 0.0, NEG)
    ones = jnp.ones((TOK, HD), jnp.bfloat16)
    for first in range(0, HEADS, STACK):
        kv_head = first // (HEADS // KVH)
        k_cols = slice(kv_head * HD, (kv_head + 1) * HD)
        v_cols = slice(KV + kv_head * HD, KV + (kv_head + 1) * HD)
        query = jnp.concatenate(
            [query_ref[0, :, h * HD : (h + 1) * HD] for h in range(first, first + STACK)], axis=0
        )
        key = jnp.concatenate([pay[:TOK, k_cols] for pay in pays], axis=0)
        scores = lax.dot_general(
            query, key, (((1,), (1,)), ((), ())), preferred_element_type=jnp.float32
        )
        bias = bias_ref[...]
        scores = scores.reshape(STACK, TOK, (SPAN + 1) * TOK) + bias[None]
        largest = jnp.max(scores, axis=-1, keepdims=True)
        weights = jnp.exp2((scores - largest) * EXP2_SCALE).astype(jnp.bfloat16)
        weights = weights.reshape(STACK * TOK, (SPAN + 1) * TOK)
        value = jnp.concatenate(
            [jnp.concatenate([pay[:TOK, v_cols], ones], axis=1) for pay in pays], axis=0
        )
        mixed = jnp.dot(weights, value, preferred_element_type=jnp.float32)
        result = (mixed[:, :HD] / mixed[:, HD:]).astype(jnp.bfloat16)
        for h in range(STACK):
            head = first + h
            rows = result[h * TOK : (h + 1) * TOK]
            out_ref[0, :, head * HD : (head + 1) * HD] = rows
            swap_ref[head // 2, :, (head % 2) * HD : (head % 2 + 1) * HD] = rows


def attend(index, queries, pays):
    return pl.pallas_call(
        attend_kernel,
        out_shape=(
            jax.ShapeDtypeStruct((1, TOK, HEADS * HD), jnp.bfloat16),
            jax.ShapeDtypeStruct((N_GROUP, TOK, WIDE), jnp.bfloat16),
        ),
        in_specs=[pl.BlockSpec(memory_space=pltpu.SMEM)] + vmem_specs(SPAN + 2),
        out_specs=tuple(vmem_specs(2)),
        scratch_shapes=[pltpu.VMEM((TOK, (SPAN + 1) * TOK), jnp.float32)],
        name="attend",
        compiler_params=pltpu.CompilerParams(vmem_limit_bytes=32 << 20),
        cost_estimate=pl.CostEstimate(
            flops=700_000_000, bytes_accessed=3 << 20, transcendentals=1_310_720
        ),
    )(index, queries, *pays)


def term_kernel(core_ref, near_ref, far_ref, mixed_ref, out_ref):
    core = core_ref[0]
    term = jnp.zeros((D_WIN, WIDE), jnp.float32)
    for x in range(N_X):
        grad = jnp.concatenate([near_ref[x], far_ref[x]], axis=1)
        mixed = jnp.concatenate([mixed_ref[2 * x + core], mixed_ref[2 * x + 1 - core]], axis=0)
        term = term + jnp.dot(grad, mixed, preferred_element_type=jnp.float32)
    term = term.astype(jnp.bfloat16).reshape(N_Y, N_ZH, 2, 2, PART, WIDE)
    for part in range(2):
        for head in range(2):
            columns = slice(head * HD, (head + 1) * HD)
            for to_core in range(2):
                for zh in range(N_ZH):
                    out_ref[2 * part + head, to_core, zh] = term[:, zh, to_core, part, :, columns]


def weight_term(core, near, far, mixed):
    return pl.pallas_call(
        term_kernel,
        out_shape=jax.ShapeDtypeStruct((N_ZL, 2, N_ZH, N_Y, PART, HD), jnp.bfloat16),
        in_specs=[pl.BlockSpec(memory_space=pltpu.SMEM)] + vmem_specs(3),
        out_specs=vmem_specs(1)[0],
        name="weight_term",
        compiler_params=params(24),
        cost_estimate=pl.CostEstimate(
            flops=2 * D_WIN * N_GROUP * TOK * WIDE, bytes_accessed=3 << 20, transcendentals=0
        ),
    )(core, near, far, mixed)


def total_kernel(terms_ref, out_ref):
    terms = terms_ref[...].reshape(N_ZL, 2, N_YZ, PART, HD)
    for core in range(2):
        own = terms[:, core].reshape(N_ZL * N_YZ, PART, HD).astype(jnp.float32)
        total = jnp.sum(own, axis=0).astype(jnp.bfloat16)
        out_ref[:, core] = jnp.broadcast_to(total[None], (N_REP, PART, HD))


def total(terms):
    return pl.pallas_call(
        total_kernel,
        out_shape=jax.ShapeDtypeStruct((N_REP, 2, PART, HD), jnp.bfloat16),
        in_specs=vmem_specs(1),
        out_specs=vmem_specs(1)[0],
        name="total",
        compiler_params=params(8),
    )(terms)


def assemble_kernel(parts_ref, out_ref):
    for x in range(N_X):
        for part in range(2):
            for half in range(2):
                for core in range(2):
                    head = 4 * x + 2 * core + half
                    piece = parts_ref[4 * x + 2 * part + half, core].astype(jnp.float32)
                    rows = slice(part * PART, (part + 1) * PART)
                    out_ref[rows, head * HD : (head + 1) * HD] = piece


def assemble(parts):
    return pl.pallas_call(
        assemble_kernel,
        out_shape=jax.ShapeDtypeStruct((D_WIN // N_SHARD, HEADS * HD), jnp.float32),
        in_specs=vmem_specs(1),
        out_specs=vmem_specs(1)[0],
        name="assemble",
        compiler_params=params(8),
    )(parts)


def step(queries, keys, values, segments, grad_output):
    core = lax.axis_index("core").astype(jnp.int32)
    index = lax.axis_index(SHARD).astype(jnp.int32)
    pay, grad_t = pack(keys, values, segments, grad_output)

    def back(steps):
        return [(s, s + steps(s)) for s in range(N_SHARD) if s + steps(s) < N_SHARD]

    def swap(value):
        return lax.ppermute(value, "core", [(0, 1), (1, 0)])

    two = lax.ppermute(pay, SHARD, back(lambda s: 2))
    near_grads = lax.all_to_all(grad_t, "x", 0, 0, tiled=True)
    near = lax.ppermute(pay, SHARD, back(lambda s: 3 if s % 2 else 1))
    four = lax.ppermute(pay, SHARD, back(lambda s: 4))
    cross = swap(two)
    attention, heads = attend(index.reshape(1), queries, [pay, two, four, near, cross])
    far_grads = swap(near_grads)
    mixed = lax.all_to_all(heads, GROUP, 0, 0, tiled=True)
    term = weight_term(core.reshape(1), near_grads, far_grads, mixed)
    terms = lax.all_to_all(
        term.reshape(N_SHARD * N_ZL, PART, HD), REST, 0, 0, tiled=True
    )
    parts = lax.all_to_all(total(terms), REP, 0, 0, tiled=True)
    return attention, assemble(parts)


def solution(mesh):
    fine = Mesh(np.asarray(mesh.devices).reshape(SIZES), AXES)
    row = P(REP, SHARD, None)
    return jax.shard_map(
        step,
        mesh=fine,
        in_specs=(row, row, row, P(REP, SHARD), row),
        out_specs=(row, P(SHARD, None)),
        check_vma=False,
    )
```

```python
import jax
import jax.numpy as jnp
import numpy as np
from jax import lax
from jax.experimental import pallas as pl
from jax.experimental.pallas import tpu as pltpu
from jax.sharding import Mesh
from jax.sharding import PartitionSpec as P


HEADS = 16
KVH = 2
HD = 128
TOK = 128
D_WIN = 1024
SPAN = 4
N_SHARD = 32
N_REP = 16
KV = KVH * HD
PAY_ROWS = TOK + 8
NEG = -1e30
EXP2_SCALE = (HD**-0.5) * 1.4426950408889634

AXES = ("x", "zl", "y", "zh", "core")
SIZES = (4, 4, 8, 2, 2)
REP = ("x", "zl")
COPIES = ("zl", "x")
SHARD = ("y", "zh", "core")
GROUP = ("x", "core")
REST = ("core", "zl", "zh", "y")
N_X = 4
N_ZL = 4
N_Y = 8
N_ZH = 2
N_YZ = N_Y * N_ZH
N_GROUP = 8
ROWS = D_WIN // N_SHARD
PART = ROWS // 2
WIDE = HEADS * HD // N_GROUP
STACK = 8


def params(mib):
    return pltpu.CompilerParams(vmem_limit_bytes=mib << 20)


def vmem_specs(count):
    return [pl.BlockSpec(memory_space=pltpu.VMEM)] * count


def pack_kernel(*refs):
    sources, (pay_out, grad_t_out), held = refs[:4], refs[4:6], refs[6:10]
    pay_ref, grad_t_ref, sems = refs[10:]
    copies = [
        pltpu.make_async_copy(source, here, sems.at[i])
        for i, (source, here) in enumerate(zip(sources, held))
    ]
    for copy in copies:
        copy.start()
    key_ref, value_ref, seg_ref, grad_ref = held
    pay_ref[TOK:, TOK:] = jnp.zeros((8, 2 * KV - TOK), jnp.bfloat16)
    for copy in copies[:3]:
        copy.wait()
    pay_ref[:TOK, :KV] = key_ref[0]
    pay_ref[:TOK, KV:] = value_ref[0]
    seg = jnp.broadcast_to(seg_ref[...].astype(jnp.float32), (8, TOK))
    pay_ref[TOK:, :TOK] = seg.astype(jnp.bfloat16)
    results = [pltpu.make_async_copy(pay_ref, pay_out, sems.at[4])]
    results[0].start()
    copies[3].wait()
    grad_t_ref[...] = jnp.transpose(grad_ref[0].astype(jnp.float32)).astype(jnp.bfloat16)
    for x in range(N_X):
        results.append(pltpu.make_async_copy(grad_t_ref, grad_t_out.at[x], sems.at[5 + x]))
        results[-1].start()
    for result in results:
        result.wait()


def pack(keys, values, segments, grad_output):
    sources = (keys, values, segments, grad_output)
    anywhere = pl.BlockSpec(memory_space=pl.ANY)
    return pl.pallas_call(
        pack_kernel,
        out_shape=(
            jax.ShapeDtypeStruct((PAY_ROWS, 2 * KV), jnp.bfloat16),
            jax.ShapeDtypeStruct((N_X, D_WIN, TOK), jnp.bfloat16),
        ),
        in_specs=[anywhere] * 4,
        out_specs=(anywhere, anywhere),
        scratch_shapes=[pltpu.VMEM(source.shape, source.dtype) for source in sources]
        + [
            pltpu.VMEM((PAY_ROWS, 2 * KV), jnp.bfloat16),
            pltpu.VMEM((D_WIN, TOK), jnp.bfloat16),
            pltpu.SemaphoreType.DMA((5 + N_X,)),
        ],
        name="pack",
        cost_estimate=pl.CostEstimate(flops=0, bytes_accessed=1 << 20, transcendentals=0),
    )(*sources)


def attend_kernel(index_ref, query_ref, *refs):
    pays, (out_ref, swap_ref, bias_ref) = refs[: SPAN + 1], refs[SPAN + 1 :]
    index = index_ref[0]
    own_row = jnp.broadcast_to(pays[0][TOK : TOK + 1, :TOK].astype(jnp.float32), (TOK, TOK))
    q_seg = jnp.transpose(own_row)
    q_at = lax.broadcasted_iota(jnp.int32, (TOK, TOK), 0)
    k_at = lax.broadcasted_iota(jnp.int32, (TOK, TOK), 1)
    for step in range(SPAN + 1):
        k_seg = jnp.broadcast_to(pays[step][TOK : TOK + 1, :TOK].astype(jnp.float32), (TOK, TOK))
        allowed = q_seg == k_seg
        if step == 0:
            allowed = allowed & (k_at <= q_at)
        else:
            odd = lax.rem(index, 2)
            back = (0, 2, 4, 3 - 2 * odd, 1 + 2 * odd)[step]
            allowed = allowed & (k_at + (index - back) * TOK >= 0)
        bias_ref[:, step * TOK : (step + 1) * TOK] = jnp.where(allowed, 0.0, NEG)
    ones = jnp.ones((TOK, HD), jnp.bfloat16)
    for first in range(0, HEADS, STACK):
        kv_head = first // (HEADS // KVH)
        k_cols = slice(kv_head * HD, (kv_head + 1) * HD)
        v_cols = slice(KV + kv_head * HD, KV + (kv_head + 1) * HD)
        query = jnp.concatenate(
            [query_ref[0, :, h * HD : (h + 1) * HD] for h in range(first, first + STACK)], axis=0
        )
        key = jnp.concatenate([pay[:TOK, k_cols] for pay in pays], axis=0)
        scores = lax.dot_general(
            query, key, (((1,), (1,)), ((), ())), preferred_element_type=jnp.float32
        )
        bias = bias_ref[...]
        scores = scores.reshape(STACK, TOK, (SPAN + 1) * TOK) + bias[None]
        largest = jnp.max(scores, axis=-1, keepdims=True)
        weights = jnp.exp2((scores - largest) * EXP2_SCALE).astype(jnp.bfloat16)
        weights = weights.reshape(STACK * TOK, (SPAN + 1) * TOK)
        value = jnp.concatenate(
            [jnp.concatenate([pay[:TOK, v_cols], ones], axis=1) for pay in pays], axis=0
        )
        mixed = jnp.dot(weights, value, preferred_element_type=jnp.float32)
        result = (mixed[:, :HD] / mixed[:, HD:]).astype(jnp.bfloat16)
        for h in range(STACK):
            head = first + h
            rows = result[h * TOK : (h + 1) * TOK]
            out_ref[0, :, head * HD : (head + 1) * HD] = rows
            swap_ref[head // 2, :, (head % 2) * HD : (head % 2 + 1) * HD] = rows


def attend(index, queries, pays):
    return pl.pallas_call(
        attend_kernel,
        out_shape=(
            jax.ShapeDtypeStruct((1, TOK, HEADS * HD), jnp.bfloat16),
            jax.ShapeDtypeStruct((N_GROUP, TOK, WIDE), jnp.bfloat16),
        ),
        in_specs=[pl.BlockSpec(memory_space=pltpu.SMEM)] + vmem_specs(SPAN + 2),
        out_specs=tuple(vmem_specs(2)),
        scratch_shapes=[pltpu.VMEM((TOK, (SPAN + 1) * TOK), jnp.float32)],
        name="attend",
        compiler_params=pltpu.CompilerParams(vmem_limit_bytes=32 << 20),
        cost_estimate=pl.CostEstimate(
            flops=700_000_000, bytes_accessed=3 << 20, transcendentals=1_310_720
        ),
    )(index, queries, *pays)


def term_kernel(core_ref, near_ref, far_ref, mixed_ref, out_ref):
    core = core_ref[0]
    term = jnp.zeros((D_WIN, WIDE), jnp.float32)
    for x in range(N_X):
        grad = jnp.concatenate([near_ref[x], far_ref[x]], axis=1)
        mixed = jnp.concatenate([mixed_ref[2 * x + core], mixed_ref[2 * x + 1 - core]], axis=0)
        term = term + jnp.dot(grad, mixed, preferred_element_type=jnp.float32)
    term = term.astype(jnp.bfloat16).reshape(N_Y, N_ZH, 2, 2, PART, WIDE)
    for part in range(2):
        for head in range(2):
            columns = slice(head * HD, (head + 1) * HD)
            for to_core in range(2):
                for zh in range(N_ZH):
                    out_ref[to_core, 2 * part + head, zh] = term[:, zh, to_core, part, :, columns]


def weight_term(core, near, far, mixed):
    return pl.pallas_call(
        term_kernel,
        out_shape=jax.ShapeDtypeStruct((2, N_ZL, N_ZH, N_Y, PART, HD), jnp.bfloat16),
        in_specs=[pl.BlockSpec(memory_space=pltpu.SMEM)] + vmem_specs(3),
        out_specs=vmem_specs(1)[0],
        name="weight_term",
        compiler_params=params(24),
        cost_estimate=pl.CostEstimate(
            flops=2 * D_WIN * N_GROUP * TOK * WIDE, bytes_accessed=3 << 20, transcendentals=0
        ),
    )(core, near, far, mixed)


def total_kernel(terms_ref, out_ref):
    terms = terms_ref[...].reshape(2, N_ZL * N_YZ, PART, HD)
    for core in range(2):
        own = terms[core].astype(jnp.float32)
        total = jnp.sum(own, axis=0).astype(jnp.bfloat16)
        out_ref[:, core] = jnp.broadcast_to(total[None], (N_REP, PART, HD))


def total(terms):
    return pl.pallas_call(
        total_kernel,
        out_shape=jax.ShapeDtypeStruct((N_REP, 2, PART, HD), jnp.bfloat16),
        in_specs=vmem_specs(1),
        out_specs=vmem_specs(1)[0],
        name="total",
        compiler_params=params(8),
    )(terms)


def assemble_kernel(parts_ref, out_ref):
    for x in range(N_X):
        for part in range(2):
            for half in range(2):
                for core in range(2):
                    head = 4 * x + 2 * core + half
                    piece = parts_ref[(2 * part + half) * N_X + x, core].astype(jnp.float32)
                    rows = slice(part * PART, (part + 1) * PART)
                    out_ref[rows, head * HD : (head + 1) * HD] = piece


def assemble(parts):
    return pl.pallas_call(
        assemble_kernel,
        out_shape=jax.ShapeDtypeStruct((D_WIN // N_SHARD, HEADS * HD), jnp.float32),
        in_specs=vmem_specs(1),
        out_specs=vmem_specs(1)[0],
        name="assemble",
        compiler_params=params(8),
    )(parts)


def step(queries, keys, values, segments, grad_output):
    core = lax.axis_index("core").astype(jnp.int32)
    index = lax.axis_index(SHARD).astype(jnp.int32)
    pay, grad_t = pack(keys, values, segments, grad_output)

    def back(steps):
        return [(s, s + steps(s)) for s in range(N_SHARD) if s + steps(s) < N_SHARD]

    def swap(value):
        return lax.ppermute(value, "core", [(0, 1), (1, 0)])

    two = lax.ppermute(pay, SHARD, back(lambda s: 2))
    near_grads = lax.all_to_all(grad_t, "x", 0, 0, tiled=True)
    near = lax.ppermute(pay, SHARD, back(lambda s: 3 if s % 2 else 1))
    four = lax.ppermute(pay, SHARD, back(lambda s: 4))
    cross = swap(two)
    attention, heads = attend(index.reshape(1), queries, [pay, two, four, near, cross])
    far_grads = swap(near_grads)
    mixed = lax.all_to_all(heads, GROUP, 0, 0, tiled=True)
    term = weight_term(core.reshape(1), near_grads, far_grads, mixed)
    terms = lax.all_to_all(
        term.reshape(N_SHARD * N_ZL, PART, HD), REST, 0, 0, tiled=True
    )
    parts = lax.all_to_all(total(terms), COPIES, 0, 0, tiled=True)
    return attention, assemble(parts)


def solution(mesh):
    fine = Mesh(np.asarray(mesh.devices).reshape(SIZES), AXES)
    row = P(REP, SHARD, None)
    return jax.shard_map(
        step,
        mesh=fine,
        in_specs=(row, row, row, P(REP, SHARD), row),
        out_specs=(row, P(SHARD, None)),
        check_vma=False,
    )
```

```python
import jax
import jax.numpy as jnp
import numpy as np
from jax import lax
from jax.experimental import pallas as pl
from jax.experimental.pallas import tpu as pltpu
from jax.sharding import Mesh
from jax.sharding import PartitionSpec as P


HEADS = 16
KVH = 2
HD = 128
TOK = 128
D_WIN = 1024
SPAN = 4
N_SHARD = 32
N_REP = 16
KV = KVH * HD
PAY_ROWS = TOK + 8
NEG = -1e30
EXP2_SCALE = (HD**-0.5) * 1.4426950408889634

AXES = ("x", "zl", "y", "zh", "core")
SIZES = (4, 4, 8, 2, 2)
REP = ("x", "zl")

SHARD = ("y", "zh", "core")
GROUP = ("x", "core")
REST = ("core", "zl", "zh", "y")
N_X = 4
N_ZL = 4
N_Y = 8
N_ZH = 2
N_YZ = N_Y * N_ZH
N_GROUP = 8
ROWS = D_WIN // N_SHARD
PART = ROWS // 2
WIDE = HEADS * HD // N_GROUP
STACK = 8


def params(mib):
    return pltpu.CompilerParams(vmem_limit_bytes=mib << 20)


def vmem_specs(count):
    return [pl.BlockSpec(memory_space=pltpu.VMEM)] * count


def pack_kernel(*refs):
    sources, (pay_out, grad_t_out), held = refs[:4], refs[4:6], refs[6:10]
    pay_ref, grad_t_ref, sems = refs[10:]
    copies = [
        pltpu.make_async_copy(source, here, sems.at[i])
        for i, (source, here) in enumerate(zip(sources, held))
    ]
    for copy in copies:
        copy.start()
    key_ref, value_ref, seg_ref, grad_ref = held
    pay_ref[TOK:, TOK:] = jnp.zeros((8, 2 * KV - TOK), jnp.bfloat16)
    for copy in copies[:3]:
        copy.wait()
    pay_ref[:TOK, :KV] = key_ref[0]
    pay_ref[:TOK, KV:] = value_ref[0]
    seg = jnp.broadcast_to(seg_ref[...].astype(jnp.float32), (8, TOK))
    pay_ref[TOK:, :TOK] = seg.astype(jnp.bfloat16)
    results = [pltpu.make_async_copy(pay_ref, pay_out, sems.at[4])]
    results[0].start()
    copies[3].wait()
    grad_t_ref[...] = jnp.transpose(grad_ref[0].astype(jnp.float32)).astype(jnp.bfloat16)
    for x in range(N_X):
        results.append(pltpu.make_async_copy(grad_t_ref, grad_t_out.at[x], sems.at[5 + x]))
        results[-1].start()
    for result in results:
        result.wait()


def pack(keys, values, segments, grad_output):
    sources = (keys, values, segments, grad_output)
    anywhere = pl.BlockSpec(memory_space=pl.ANY)
    return pl.pallas_call(
        pack_kernel,
        out_shape=(
            jax.ShapeDtypeStruct((PAY_ROWS, 2 * KV), jnp.bfloat16),
            jax.ShapeDtypeStruct((N_X, D_WIN, TOK), jnp.bfloat16),
        ),
        in_specs=[anywhere] * 4,
        out_specs=(anywhere, anywhere),
        scratch_shapes=[pltpu.VMEM(source.shape, source.dtype) for source in sources]
        + [
            pltpu.VMEM((PAY_ROWS, 2 * KV), jnp.bfloat16),
            pltpu.VMEM((D_WIN, TOK), jnp.bfloat16),
            pltpu.SemaphoreType.DMA((5 + N_X,)),
        ],
        name="pack",
        cost_estimate=pl.CostEstimate(flops=0, bytes_accessed=1 << 20, transcendentals=0),
    )(*sources)


def attend_kernel(index_ref, query_ref, *refs):
    pays, (out_ref, swap_ref, bias_ref) = refs[: SPAN + 1], refs[SPAN + 1 :]
    index = index_ref[0]
    own_row = jnp.broadcast_to(pays[0][TOK : TOK + 1, :TOK].astype(jnp.float32), (TOK, TOK))
    q_seg = jnp.transpose(own_row)
    q_at = lax.broadcasted_iota(jnp.int32, (TOK, TOK), 0)
    k_at = lax.broadcasted_iota(jnp.int32, (TOK, TOK), 1)
    for step in range(SPAN + 1):
        k_seg = jnp.broadcast_to(pays[step][TOK : TOK + 1, :TOK].astype(jnp.float32), (TOK, TOK))
        allowed = q_seg == k_seg
        if step == 0:
            allowed = allowed & (k_at <= q_at)
        else:
            odd = lax.rem(index, 2)
            back = (0, 2, 4, 3 - 2 * odd, 1 + 2 * odd)[step]
            allowed = allowed & (k_at + (index - back) * TOK >= 0)
        bias_ref[:, step * TOK : (step + 1) * TOK] = jnp.where(allowed, 0.0, NEG)
    ones = jnp.ones((TOK, HD), jnp.bfloat16)
    for first in range(0, HEADS, STACK):
        kv_head = first // (HEADS // KVH)
        k_cols = slice(kv_head * HD, (kv_head + 1) * HD)
        v_cols = slice(KV + kv_head * HD, KV + (kv_head + 1) * HD)
        query = jnp.concatenate(
            [query_ref[0, :, h * HD : (h + 1) * HD] for h in range(first, first + STACK)], axis=0
        )
        key = jnp.concatenate([pay[:TOK, k_cols] for pay in pays], axis=0)
        scores = lax.dot_general(
            query, key, (((1,), (1,)), ((), ())), preferred_element_type=jnp.float32
        )
        bias = bias_ref[...]
        scores = scores.reshape(STACK, TOK, (SPAN + 1) * TOK) + bias[None]
        largest = jnp.max(scores, axis=-1, keepdims=True)
        weights = jnp.exp2((scores - largest) * EXP2_SCALE).astype(jnp.bfloat16)
        weights = weights.reshape(STACK * TOK, (SPAN + 1) * TOK)
        value = jnp.concatenate(
            [jnp.concatenate([pay[:TOK, v_cols], ones], axis=1) for pay in pays], axis=0
        )
        mixed = jnp.dot(weights, value, preferred_element_type=jnp.float32)
        result = (mixed[:, :HD] / mixed[:, HD:]).astype(jnp.bfloat16)
        for h in range(STACK):
            head = first + h
            rows = result[h * TOK : (h + 1) * TOK]
            out_ref[0, :, head * HD : (head + 1) * HD] = rows
            swap_ref[head // 2, :, (head % 2) * HD : (head % 2 + 1) * HD] = rows


def attend(index, queries, pays):
    return pl.pallas_call(
        attend_kernel,
        out_shape=(
            jax.ShapeDtypeStruct((1, TOK, HEADS * HD), jnp.bfloat16),
            jax.ShapeDtypeStruct((N_GROUP, TOK, WIDE), jnp.bfloat16),
        ),
        in_specs=[pl.BlockSpec(memory_space=pltpu.SMEM)] + vmem_specs(SPAN + 2),
        out_specs=tuple(vmem_specs(2)),
        scratch_shapes=[pltpu.VMEM((TOK, (SPAN + 1) * TOK), jnp.float32)],
        name="attend",
        compiler_params=pltpu.CompilerParams(vmem_limit_bytes=32 << 20),
        cost_estimate=pl.CostEstimate(
            flops=700_000_000, bytes_accessed=3 << 20, transcendentals=1_310_720
        ),
    )(index, queries, *pays)


def term_kernel(core_ref, near_ref, far_ref, mixed_ref, out_ref):
    core = core_ref[0]
    term = jnp.zeros((D_WIN, WIDE), jnp.float32)
    for x in range(N_X):
        grad = jnp.concatenate([near_ref[x], far_ref[x]], axis=1)
        mixed = jnp.concatenate([mixed_ref[2 * x + core], mixed_ref[2 * x + 1 - core]], axis=0)
        term = term + jnp.dot(grad, mixed, preferred_element_type=jnp.float32)
    term = term.astype(jnp.bfloat16).reshape(N_Y, N_ZH, 2, 2, PART, WIDE)
    for part in range(2):
        for head in range(2):
            columns = slice(head * HD, (head + 1) * HD)
            for to_core in range(2):
                for zh in range(N_ZH):
                    out_ref[to_core, 2 * part + head, zh] = term[:, zh, to_core, part, :, columns]


def weight_term(core, near, far, mixed):
    return pl.pallas_call(
        term_kernel,
        out_shape=jax.ShapeDtypeStruct((2, N_ZL, N_ZH, N_Y, PART, HD), jnp.bfloat16),
        in_specs=[pl.BlockSpec(memory_space=pltpu.SMEM)] + vmem_specs(3),
        out_specs=vmem_specs(1)[0],
        name="weight_term",
        compiler_params=params(24),
        cost_estimate=pl.CostEstimate(
            flops=2 * D_WIN * N_GROUP * TOK * WIDE, bytes_accessed=3 << 20, transcendentals=0
        ),
    )(core, near, far, mixed)


def total_kernel(terms_ref, out_ref):
    terms = terms_ref[...].reshape(2, N_ZL * N_YZ, PART, HD)
    for core in range(2):
        own = terms[core].astype(jnp.float32)
        total = jnp.sum(own, axis=0).astype(jnp.bfloat16)
        out_ref[:, core] = jnp.broadcast_to(total[None], (N_REP, PART, HD))


def total(terms):
    return pl.pallas_call(
        total_kernel,
        out_shape=jax.ShapeDtypeStruct((N_REP, 2, PART, HD), jnp.bfloat16),
        in_specs=vmem_specs(1),
        out_specs=vmem_specs(1)[0],
        name="total",
        compiler_params=params(8),
    )(terms)


def assemble_kernel(parts_ref, out_ref):
    for x in range(N_X):
        for part in range(2):
            for half in range(2):
                for core in range(2):
                    head = 4 * x + 2 * core + half
                    piece = parts_ref[4 * x + 2 * part + half, core].astype(jnp.float32)
                    rows = slice(part * PART, (part + 1) * PART)
                    out_ref[rows, head * HD : (head + 1) * HD] = piece


def assemble(parts):
    return pl.pallas_call(
        assemble_kernel,
        out_shape=jax.ShapeDtypeStruct((D_WIN // N_SHARD, HEADS * HD), jnp.float32),
        in_specs=vmem_specs(1),
        out_specs=vmem_specs(1)[0],
        name="assemble",
        compiler_params=params(8),
    )(parts)


def step(queries, keys, values, segments, grad_output):
    core = lax.axis_index("core").astype(jnp.int32)
    index = lax.axis_index(SHARD).astype(jnp.int32)
    pay, grad_t = pack(keys, values, segments, grad_output)

    def back(steps):
        return [(s, s + steps(s)) for s in range(N_SHARD) if s + steps(s) < N_SHARD]

    def swap(value):
        return lax.ppermute(value, "core", [(0, 1), (1, 0)])

    two = lax.ppermute(pay, SHARD, back(lambda s: 2))
    near_grads = lax.all_to_all(grad_t, "x", 0, 0, tiled=True)
    near = lax.ppermute(pay, SHARD, back(lambda s: 3 if s % 2 else 1))
    four = lax.ppermute(pay, SHARD, back(lambda s: 4))
    cross = swap(two)
    attention, heads = attend(index.reshape(1), queries, [pay, two, four, near, cross])
    far_grads = swap(near_grads)
    mixed = lax.all_to_all(heads, GROUP, 0, 0, tiled=True)
    term = weight_term(core.reshape(1), near_grads, far_grads, mixed)
    terms = lax.all_to_all(
        term.reshape(N_SHARD * N_ZL, PART, HD), REST, 0, 0, tiled=True
    )
    parts = lax.all_to_all(total(terms), REP, 0, 0, tiled=True)
    return attention, assemble(parts)


def solution(mesh):
    fine = Mesh(np.asarray(mesh.devices).reshape(SIZES), AXES)
    row = P(REP, SHARD, None)
    return jax.shard_map(
        step,
        mesh=fine,
        in_specs=(row, row, row, P(REP, SHARD), row),
        out_specs=(row, P(SHARD, None)),
        check_vma=False,
    )
```
